1024 devices in a mesh: cells: 128 (over z, y, core), states: 8 (over x).
Axes of the slice: x: 8, y: 8, z: 8, core: 2. Of those that a mesh axis runs over, the one named last changes fastest.
Arguments:
- filter_input: bfloat16 [81536, 1024], P('cells', 'states'), may hold values from -4 to 4, as said below
- cell_table: bfloat16 [8, 343, 343], replicated, may hold values from -0.5 to 3.5, as said below
- cell_type: int32 [256], P('cells'), may hold values from 0 to 7
- atom_center: int32 [512], P('cells'), may hold values from 0 to 1, as said below
- proj_values: bfloat16 [512, 3, 16, 343], P('cells'), may hold values from -0.3125 to 0.3125
- coupling: float32 [16, 16], replicated, may hold values from -1.5 to 1.5
- occupation: float32 [1024], P('states'), may hold values from 0.25 to 4
Outputs:
- filtered: float32 [81536, 1024], P('cells', 'states')
- density: float32 [81536], P('cells')
The draws below stay inside these ranges and needn't reach their ends.
Inputs may be any that keep to these rules, and one draw needn't show every extreme that they name: `filter_input`: rows that stand for the same node on two blocks hold the same values. `cell_table`: each of the 8 matrices is symmetric. `atom_center`: in each block of 4 atoms of one owner, at least one atom sits on cell 0 and at least one on cell 1.
All inputs are finite; a program needn't handle non-finite values.
Results may differ from the reference program's by a relative error of at most 0.0027.
Values may be sent and summed in bfloat16 or wider, within the bound.
A program may use at most 32 MiB of HBM per device.

```python
import math
import jax
import jax.numpy as jnp
from jax import lax

CELL_DEV = 2
STATE_DEV = 128
NTYPE = 8
ATOM_DEV = 4
PROJECTORS = 16
STEPS = 3
FACE = 49
CELL_NODES = 343
STRIDE = 294
NODE_DEV = 637
CELLS = 256
NODES = 81536
STATES = 1024
ATOMS = 512
N_CELLS = 128
N_STATES = 8


def draw_filter_input(key, part):
    total_rows = N_CELLS * CELL_DEV * STRIDE
    values = jnp.clip(jax.random.normal(key, (total_rows, STATES), jnp.float32), -4.0, 4.0)
    blocks = values.reshape(N_CELLS, CELL_DEV * STRIDE, STATES)
    following = jnp.roll(blocks, -1, axis=0)[:, :FACE]
    return jnp.concatenate([blocks, following], axis=1).reshape(NODES, STATES).astype(jnp.bfloat16)


def draw_cell_table(key, part):
    first, second = jax.random.split(key)
    shape = (NTYPE, CELL_NODES, CELL_NODES)
    noise = jnp.clip(jax.random.normal(first, shape, jnp.float32), -5.0, 5.0)
    symmetric = (noise + jnp.swapaxes(noise, 1, 2)) * (0.5 / math.sqrt(CELL_NODES))
    diagonal = jax.random.uniform(second, (NTYPE, CELL_NODES), jnp.float32, 1.0, 3.0)
    eye = jnp.eye(CELL_NODES, dtype=jnp.float32)
    table = symmetric * (1.0 - eye)[None] + diagonal[:, :, None] * eye[None]
    return table.astype(jnp.bfloat16)


def draw_atom_center(key, part):
    first, second = jax.random.split(jax.random.fold_in(key, 17))
    base = jax.random.randint(first, (N_CELLS, ATOM_DEV), 0, CELL_DEV, dtype=jnp.int32)
    slot_keys = jax.random.split(second, N_CELLS)
    slots = jax.vmap(lambda k: jax.random.permutation(k, ATOM_DEV))(slot_keys).astype(jnp.int32)
    centers = jnp.where(slots == 0, 0, jnp.where(slots == 1, CELL_DEV - 1, base))
    return centers.reshape(ATOMS).astype(jnp.int32)


def with_ends(entries, stream_key, least, top_value):
    longest = entries.shape.index(max(entries.shape))
    spots = []
    for shift in (0, 1):
        where = [jax.random.randint(jax.random.fold_in(stream_key, axis), (), 0, length) for axis, length in enumerate(entries.shape)]
        where[longest] = (where[longest] + shift) % entries.shape[longest]
        spots.append(tuple(where))
    return entries.at[spots[0]].set(least).at[spots[1]].set(top_value)


def steps_of(rng, extent, pieces, smallest, largest):
    loudness = 1.0
    for dim, blocks in pieces:
        draws = jax.random.uniform(jax.random.fold_in(jax.random.fold_in(rng, 6), dim), (blocks,), jnp.float32, smallest / len(pieces), largest / len(pieces))
        loudness = loudness * jnp.repeat(jnp.exp(draws), extent[dim] // blocks).reshape((-1,) + (1,) * (len(extent) - 1 - dim))
    return loudness


def gaussian(stream_key, extent, scale, most, cuts=(), held_as=jnp.bfloat16):
    entries = scale * jax.random.normal(stream_key, extent, jnp.float32)
    if cuts:
        entries = entries * steps_of(stream_key, extent, cuts, -0.22, 0.18)
    return jnp.clip(entries, -most, most).astype(held_as)


def setup_inputs(seed: int = 0) -> dict:
    key_of = jax.random.split(jax.random.key(seed), 8)
    filter_input = draw_filter_input(jax.random.fold_in(key_of[7], 71), 0)
    cell_table = draw_cell_table(jax.random.fold_in(key_of[7], 71), 0)
    cell_type = with_ends(jax.random.randint(key_of[2], (CELLS,), 0, NTYPE), jax.random.fold_in(key_of[2], 1), 0, NTYPE - 1).astype(jnp.int32)
    atom_center = draw_atom_center(jax.random.fold_in(key_of[7], 71), 0)
    proj_values = gaussian(key_of[4], (ATOMS, 3, PROJECTORS, CELL_NODES), CELL_NODES ** -0.5, 0.3125, ((0, 128),))
    coupling = gaussian(key_of[5], (PROJECTORS, PROJECTORS), PROJECTORS ** -0.5, 1.5, (), jnp.float32)
    occupation = jnp.clip(jnp.exp(math.log(4.0) - 2.7725887 * jax.random.uniform(key_of[6], (STATES,), jnp.float32) ** steps_of(key_of[6], (STATES,), ((0, 8),), -0.2, 0.2)), 0.25, 4.0)
    return {"filter_input": filter_input, "cell_table": cell_table, "cell_type": cell_type, "atom_center": atom_center, "proj_values": proj_values, "coupling": coupling, "occupation": occupation}


lower_edge = 4.0
upper_edge = 12.0
ground_edge = -2.0


def split_cells(node_block):
    tile_count = (node_block.shape[0] - FACE) // STRIDE
    columns = node_block.shape[1]
    head_rows = node_block[: tile_count * STRIDE].reshape(tile_count, STRIDE, columns)
    padded = jnp.pad(node_block, ((0, STRIDE - FACE), (0, 0)))
    face_rows = padded[STRIDE: STRIDE + tile_count * STRIDE].reshape(tile_count, STRIDE, columns)[:, :FACE]
    return jnp.concatenate([head_rows, face_rows], axis=1)


def join_cells(cell_tiles):
    tile_count = cell_tiles.shape[0]
    columns = cell_tiles.shape[2]
    head_rows = cell_tiles[:, :STRIDE].reshape(tile_count * STRIDE, columns)
    tail_rows = jnp.pad(cell_tiles[:, STRIDE:], ((0, 0), (0, STRIDE - FACE), (0, 0))).reshape(tile_count * STRIDE, columns)
    return jnp.pad(head_rows, ((0, FACE), (0, 0))) + jnp.pad(tail_rows, ((STRIDE, 0), (0, 0)))[: tile_count * STRIDE + FACE]


def apply_cycle(current, cell_table, cell_type, atom_center, proj_values, coupling):
    rounded = current.astype(jnp.bfloat16)
    closed = jnp.concatenate([rounded, rounded[:FACE]], axis=0)
    tiles = split_cells(closed).reshape(N_CELLS, CELL_DEV, CELL_NODES, -1)
    types = cell_type.reshape(N_CELLS, CELL_DEV)

    def cell_block(inputs_pair):
        tile_block, type_block = inputs_pair
        matrices = jnp.take(cell_table, type_block, axis=0).astype(jnp.float32)
        return jnp.einsum("cij,cjs->cis", matrices, tile_block.astype(jnp.float32), precision=lax.Precision.HIGHEST)

    cell_terms = lax.map(cell_block, (tiles, types))
    extended = jnp.concatenate([jnp.roll(tiles, 1, axis=0)[:, -1:], tiles, jnp.roll(tiles, -1, axis=0)[:, :1]], axis=1)
    centers = atom_center.reshape(N_CELLS, ATOM_DEV)
    values = proj_values.reshape(N_CELLS, ATOM_DEV, 3, PROJECTORS, CELL_NODES)

    def atom_block(inputs_triple):
        ext_block, center_block, value_block = inputs_triple
        picks = center_block[:, None] + jnp.arange(3, dtype=jnp.int32)[None, :]
        onehot = (picks[:, :, None] == jnp.arange(CELL_DEV + 2, dtype=jnp.int32)[None, None, :]).astype(jnp.float32)
        beta_cells = jnp.einsum("ajk,ajpr->kapr", onehot, value_block.astype(jnp.float32), precision=lax.Precision.HIGHEST)
        beta_cells = beta_cells.reshape(CELL_DEV + 2, ATOM_DEV * PROJECTORS, CELL_NODES)
        coeffs = jnp.einsum("kqr,krs->qs", beta_cells, ext_block.astype(jnp.float32), precision=lax.Precision.HIGHEST)
        weighted = jnp.einsum("pq,aqs->aps", coupling, coeffs.reshape(ATOM_DEV, PROJECTORS, -1), precision=lax.Precision.HIGHEST)
        weighted = weighted.astype(jnp.bfloat16).astype(jnp.float32).reshape(ATOM_DEV * PROJECTORS, -1)
        return jnp.einsum("kqr,qs->krs", beta_cells, weighted, precision=lax.Precision.HIGHEST)

    spread = lax.map(atom_block, (extended, centers, values))
    total = cell_terms + spread[:, 1:-1]
    total = total.at[:, 0].add(jnp.roll(spread[:, -1], 1, axis=0))
    total = total.at[:, -1].add(jnp.roll(spread[:, 0], -1, axis=0))
    opened = join_cells(total.reshape(CELLS, CELL_NODES, -1))
    return opened[:-FACE] + jnp.pad(opened[-FACE:], ((0, CELLS * STRIDE - FACE), (0, 0)))


def filter_block(columns, cell_table, cell_type, atom_center, proj_values, coupling):
    half_width = (upper_edge - lower_edge) / 2.0
    centre = (upper_edge + lower_edge) / 2.0
    scale_now = half_width / (ground_edge - centre)
    twice_inverse = 2.0 / scale_now
    previous = columns.astype(jnp.float32)
    current = (apply_cycle(previous, cell_table, cell_type, atom_center, proj_values, coupling) - centre * previous) * (scale_now / half_width)
    for repeat in range(STEPS - 1):
        scale_next = 1.0 / (twice_inverse - scale_now)
        image = apply_cycle(current, cell_table, cell_type, atom_center, proj_values, coupling)
        upcoming = (image - centre * current) * (2.0 * scale_next / half_width) - (scale_now * scale_next) * previous
        previous, current = current, upcoming
        scale_now = scale_next
    return current


def lay_out(node_rows):
    blocks = node_rows.reshape((N_CELLS, CELL_DEV * STRIDE) + node_rows.shape[1:])
    following = jnp.roll(blocks, -1, axis=0)[:, :FACE]
    return jnp.concatenate([blocks, following], axis=1).reshape((NODES,) + node_rows.shape[1:])


def reference(filter_input, cell_table, cell_type, atom_center, proj_values, coupling, occupation):
    owned = filter_input.reshape(N_CELLS, NODE_DEV, STATES)[:, : CELL_DEV * STRIDE]
    owned = owned.reshape(CELLS * STRIDE, N_STATES, STATE_DEV)
    by_block = jnp.transpose(owned, (1, 0, 2))
    weights = occupation.reshape(N_STATES, STATE_DEV)

    def one_block(inputs_pair):
        columns, occ_block = inputs_pair
        result = filter_block(columns, cell_table, cell_type, atom_center, proj_values, coupling)
        return result, jnp.sum(result * result * occ_block[None, :], axis=1)

    results, partial_density = lax.map(one_block, (by_block, weights))
    filtered_rows = jnp.transpose(results, (1, 0, 2)).reshape(CELLS * STRIDE, STATES)
    density_rows = jnp.sum(partial_density, axis=0) / STATES
    return lay_out(filtered_rows), lay_out(density_rows)
```

```python
import functools

import jax
import jax.numpy as jnp
from jax import lax
from jax.experimental import pallas as pl
from jax.experimental.pallas import tpu as pltpu
from jax.sharding import PartitionSpec as P

PROJECTORS = 16
STEPS = 3
FACE = 49
CELL_NODES = 343
STRIDE = 294
CELL_DEV = 2
NTYPE = 8
ATOM_DEV = 4
NODE_DEV = 637
STATE_DEV = 128
COEFS = ATOM_DEV * PROJECTORS

lower_edge = 4.0
upper_edge = 12.0
ground_edge = -2.0

DEPTH = 384
ROWS = 352
FIELD = 688
TAIL = 288
TAIL_SKIP = STRIDE - TAIL
TAIL_COL = 256
FACE_PAD = 56

BF = jnp.bfloat16
F32 = jnp.float32
LINK = jnp.float32
MESH = pl.DeviceIdType.MESH


def mm(a, b):
    return jnp.dot(a, b, preferred_element_type=F32)


def mm_nt(a, b):
    return lax.dot_general(a, b, (((1,), (1,)), ((), ())), preferred_element_type=F32)


def scales():
    half_width = (upper_edge - lower_edge) / 2.0
    scale_now = half_width / (ground_edge - (upper_edge + lower_edge) / 2.0)
    twice_inverse = 2.0 / scale_now
    pairs = [(scale_now / half_width, 0.0)]
    for _ in range(STEPS - 1):
        scale_next = 1.0 / (twice_inverse - scale_now)
        pairs.append((2.0 * scale_next / half_width, scale_now * scale_next))
        scale_now = scale_next
    return pairs


def kernel(
    nc,
    ns,
    x_hbm,
    tab_hbm,
    type_ref,
    center_ref,
    proj_hbm,
    coup_ref,
    occ_ref,
    out_x,
    out_d,
    xin,
    tab,
    proj,
    hwide,
    hmat,
    own,
    ends_send,
    ends_recv,
    spread_mat,
    face_wide,
    face_mat,
    mix,
    field,
    last,
    own_send,
    own_recv,
    side_send,
    side_recv,
    dens_send,
    dens_recv,
    load_sem,
    ends_sems,
    own_sems,
    near_sems,
    far_sems,
    dens_sems,
):
    here = lax.axis_index("cells")
    column = lax.axis_index("states")

    def cell_at(shift):
        return {"cells": lax.rem(here + (shift + nc), nc)}

    def state_at(shift):
        return {"states": lax.rem(column + shift, ns)}

    barrier = pltpu.get_barrier_semaphore()
    for shift in (-2, -1, 1, 2):
        pl.semaphore_signal(barrier, inc=1, device_id=cell_at(shift), device_id_type=MESH)
    for shift in range(1, ns):
        pl.semaphore_signal(barrier, inc=1, device_id=state_at(shift), device_id_type=MESH)

    loads = [
        pltpu.make_async_copy(proj_hbm, proj, load_sem.at[0]),
        pltpu.make_async_copy(x_hbm, xin, load_sem.at[1]),
        pltpu.make_async_copy(tab_hbm, tab, load_sem.at[2]),
    ]
    for load in loads:
        load.start()

    own[...] = jnp.zeros_like(own)
    dens_send[...] = jnp.zeros_like(dens_send)
    ends_send[...] = jnp.zeros_like(ends_send)
    field[:, NODE_DEV - 5 :, :] = jnp.zeros((STEPS, FIELD - NODE_DEV + 5, STATE_DEV), F32)
    hwide[...] = jnp.zeros_like(hwide)

    loads[0].wait()
    for atom in range(ATOM_DEV):
        first = center_ref[atom] == 0
        rows = pl.ds(atom * PROJECTORS, PROJECTORS)
        before, middle, after = (proj[atom, j].astype(F32) for j in range(3))
        zero = jnp.zeros_like(before)
        on_first = jnp.where(first, middle, before).astype(BF)
        on_second = jnp.where(first, after, middle).astype(BF)
        own[0, rows, :CELL_NODES] = on_first
        own[1, rows, :CELL_NODES] = on_second
        ends_send[0, rows, :CELL_NODES] = jnp.where(first, before, zero).astype(BF)
        ends_send[1, rows, :CELL_NODES] = jnp.where(first, zero, after).astype(BF)
    ends_send[0, :, DEPTH:] = own[0, :, :128]
    ends_send[1, :, DEPTH:] = own[1, :, TAIL_COL:]

    coup = coup_ref[...]
    high = coup.astype(BF)
    low = (coup - high.astype(F32)).astype(BF)
    many = 3 * COEFS
    pick = (
        lax.rem(lax.broadcasted_iota(jnp.int32, (many, PROJECTORS), 0), PROJECTORS)
        == lax.broadcasted_iota(jnp.int32, (many, PROJECTORS), 1)
    )
    pick = jnp.where(pick, 1.0, 0.0).astype(BF)
    same = lax.div(lax.broadcasted_iota(jnp.int32, (many, many), 0), PROJECTORS) == lax.div(
        lax.broadcasted_iota(jnp.int32, (many, many), 1), PROJECTORS
    )
    for index, piece in enumerate((high, low)):
        wide = mm_nt(mm(pick, piece).astype(BF), pick)
        mix[index] = jnp.where(same, wide, 0.0).astype(BF)

    pl.semaphore_wait(barrier, 4 + ns - 1)

    def send(src, dst, sems, slot, device):
        copy = pltpu.make_async_remote_copy(
            src_ref=src,
            dst_ref=dst,
            send_sem=sems.at[0, slot],
            recv_sem=sems.at[1, slot],
            device_id=device,
            device_id_type=MESH,
        )
        copy.start()
        return copy

    ends = [
        send(ends_send.at[0], ends_recv.at[1], ends_sems, 0, cell_at(-1)),
        send(ends_send.at[1], ends_recv.at[0], ends_sems, 1, cell_at(1)),
    ]

    loads[1].wait()
    field[0, :NODE_DEV, :] = xin[...].astype(F32)

    loads[2].wait()
    chunk = 256 // NTYPE
    spot = lax.broadcasted_iota(jnp.int32, (CELL_DEV * chunk, 256), 0)
    kind = jnp.where(spot < chunk, type_ref[0], type_ref[1])
    take = lax.broadcasted_iota(jnp.int32, (CELL_DEV * chunk, 256), 1) == lax.rem(spot, chunk) * NTYPE + kind
    take = jnp.where(take, 1.0, 0.0).astype(BF)
    for start in range(0, CELL_NODES, chunk):
        count = min(chunk, CELL_NODES - start)
        entries = tab[start : start + count].reshape(count * NTYPE, CELL_NODES)
        rows = mm(take[:, : count * NTYPE], entries)
        for cell in range(CELL_DEV):
            hwide[cell, start : start + count, :CELL_NODES] = rows[cell * chunk : cell * chunk + count]
    hmat[...] = hwide[...].astype(BF)

    pending = []
    for step, (gain, back) in enumerate(scales()):
        x = field.at[step]
        first_cell = x[:DEPTH, :].astype(BF)
        second_cell = x[STRIDE : STRIDE + DEPTH, :].astype(BF)

        mine = mm(own[0], first_cell) + mm(own[1], second_cell)
        face_first = mm(hmat[0, :64, :], first_cell)
        face_second = mm(hmat[1, TAIL : TAIL + 64, :], second_cell)
        own_send[step, 0, :COEFS, :] = mine.astype(LINK)
        own_send[step, 1, :COEFS, :] = mine.astype(LINK)
        own_send[step, 0, COEFS:, :] = face_first[:FACE_PAD].astype(LINK)
        own_send[step, 1, COEFS:, :] = face_second[:FACE_PAD].astype(LINK)
        own_copies = [
            send(own_send.at[step, 0], own_recv.at[step, 1], own_sems.at[step], 0, cell_at(-1)),
            send(own_send.at[step, 1], own_recv.at[step, 0], own_sems.at[step], 1, cell_at(1)),
        ]

        if step == 0:
            for copy in ends:
                copy.wait_recv()
        before = mm(ends_recv[0, :, :DEPTH], first_cell)
        after = mm(ends_recv[1, :, :DEPTH], second_cell)
        side_send[step, 0] = before.astype(LINK)
        side_send[step, 1] = after.astype(LINK)
        far_copies = [
            send(side_send.at[step, 0], side_recv.at[step, 1, 1], far_sems.at[step], 0, cell_at(-2)),
            send(side_send.at[step, 1], side_recv.at[step, 0, 1], far_sems.at[step], 1, cell_at(2)),
        ]
        near_copies = [
            send(side_send.at[step, 0], side_recv.at[step, 1, 0], near_sems.at[step], 0, cell_at(-1)),
            send(side_send.at[step, 1], side_recv.at[step, 0, 0], near_sems.at[step], 1, cell_at(1)),
        ]
        copies = own_copies + far_copies + near_copies
        pending += copies

        target = last if step == STEPS - 1 else field.at[step + 1]
        centre = (upper_edge + lower_edge) / 2.0
        base = (-centre * gain) * x[:NODE_DEV, :]
        if step:
            base = base - back * field[step - 1, :NODE_DEV, :]
        target[:NODE_DEV, :] = base
        target[:CELL_NODES, :] += gain * mm(hmat[0], first_cell)[:CELL_NODES]
        target[STRIDE:NODE_DEV, :] += gain * mm(hmat[1], second_cell)[:CELL_NODES]

        if step == 0:
            spread_mat[0] = jnp.concatenate([ends_recv[0, :, :DEPTH], own[0]], axis=0).astype(F32).T.astype(BF)
            spread_mat[1] = jnp.concatenate([own[1], ends_recv[1, :, :DEPTH]], axis=0).astype(F32).T.astype(BF)
            face_wide[0] = jnp.concatenate(
                [ends_recv[0, :, DEPTH:], ends_send[0, :, TAIL_COL:DEPTH]], axis=0
            ).astype(F32).T
            face_wide[1] = jnp.concatenate(
                [ends_send[1, :, :128], ends_recv[1, :, DEPTH:]], axis=0
            ).astype(F32).T
            skip = STRIDE - TAIL_COL
            face_mat[0] = face_wide[0, skip : skip + FACE_PAD, :].astype(BF)
            face_mat[1] = face_wide[1, :FACE_PAD, :].astype(BF)

        for copy in copies:
            copy.wait_recv()
        got = own_recv[step].astype(F32)
        sides = side_recv[step].astype(F32)
        coeffs = jnp.concatenate(
            [
                before + got[0, :COEFS] + sides[0, 1],
                mine + sides[0, 0] + sides[1, 0],
                after + got[1, :COEFS] + sides[1, 1],
            ],
            axis=0,
        )
        high = coeffs.astype(BF)
        low = (coeffs - high.astype(F32)).astype(BF)
        weighted = (mm(mix[0], high) + mm(mix[1], high) + mm(mix[0], low)).astype(BF)
        left, right = weighted[: 2 * COEFS], weighted[COEFS:]
        target[:CELL_NODES, :] += gain * mm(spread_mat[0], left)[:CELL_NODES]
        target[STRIDE:NODE_DEV, :] += gain * mm(spread_mat[1], right)[:CELL_NODES]
        skip = COEFS + TAIL_SKIP
        target[:FACE, :] += gain * (
            mm(face_mat[0], left)[:FACE] + own_recv[step, 0, skip : skip + FACE, :].astype(F32)
        )
        target[NODE_DEV - FACE : NODE_DEV, :] += gain * (
            mm(face_mat[1], right)[:FACE] + own_recv[step, 1, COEFS : COEFS + FACE, :].astype(F32)
        )

    store = pltpu.make_async_copy(last, out_x, load_sem.at[0])
    store.start()

    square = last[...] * last[...]
    high = square.astype(BF)
    low = (square - high.astype(F32)).astype(BF)
    weight = occ_ref[...] * (1.0 / (STATE_DEV * ns))
    weight_high = weight.astype(BF).astype(F32)
    row = lax.broadcasted_iota(jnp.int32, (16, STATE_DEV), 0)
    weights = jnp.where(row == 0, weight_high, jnp.where(row == 1, weight - weight_high, 0.0)).astype(BF)
    sums = mm_nt(weights, high) + mm_nt(weights, low)
    sums = sums[0:1] + sums[1:2]
    tiles = dens_send.shape[0]
    for tile in range(tiles):
        end = min(NODE_DEV, (tile + 1) * 128)
        dens_send[tile : tile + 1, : end - tile * 128] = sums[:, tile * 128 : end]
    dens_recv[column] = dens_send[...]
    dens_copies = []
    for shift in sorted(range(1, ns), key=lambda k: -min(k, ns - k)):
        dens_copies.append(send(dens_send, dens_recv.at[column], dens_sems, shift - 1, state_at(shift)))
    for copy in dens_copies:
        copy.wait_recv()
    total = dens_recv[0]
    for peer in range(1, ns):
        total = total + dens_recv[peer]
    for tile in range(tiles):
        end = min(NODE_DEV, (tile + 1) * 128)
        out_d[tile * 128 : end] = total[tile, : end - tile * 128]

    for copy in ends + pending + dens_copies:
        copy.wait_send()
    store.wait()


def solution(mesh):
    nc, ns = mesh.shape["cells"], mesh.shape["states"]

    def body(filter_input, cell_table, cell_type, atom_center, proj_values, coupling, occupation):
        any_space = pl.BlockSpec(memory_space=pl.ANY)
        vmem = pl.BlockSpec(memory_space=pltpu.VMEM)
        smem = pl.BlockSpec(memory_space=pltpu.SMEM)
        dma = pltpu.SemaphoreType.DMA
        filtered, density = pl.pallas_call(
            functools.partial(kernel, nc, ns),
            out_shape=(
                jax.ShapeDtypeStruct((NODE_DEV, STATE_DEV), F32),
                jax.ShapeDtypeStruct((NODE_DEV,), F32),
            ),
            in_specs=[any_space, any_space, smem, smem, any_space, vmem, vmem],
            out_specs=(any_space, vmem),
            scratch_shapes=[
                pltpu.VMEM((NODE_DEV, STATE_DEV), BF),
                pltpu.VMEM((CELL_NODES, NTYPE, CELL_NODES), BF),
                pltpu.VMEM(proj_values.shape, BF),
                pltpu.VMEM((CELL_DEV, ROWS, DEPTH), F32),
                pltpu.VMEM((CELL_DEV, ROWS, DEPTH), BF),
                pltpu.VMEM((CELL_DEV, COEFS, DEPTH), BF),
                pltpu.VMEM((2, COEFS, DEPTH + 128), BF),
                pltpu.VMEM((2, COEFS, DEPTH + 128), BF),
                pltpu.VMEM((2, DEPTH, 2 * COEFS), BF),
                pltpu.VMEM((2, 128, 2 * COEFS), F32),
                pltpu.VMEM((2, FACE_PAD, 2 * COEFS), BF),
                pltpu.VMEM((2, 3 * COEFS, 3 * COEFS), BF),
                pltpu.VMEM((STEPS, FIELD, STATE_DEV), F32),
                pltpu.VMEM((NODE_DEV, STATE_DEV), F32),
                pltpu.VMEM((STEPS, 2, COEFS + FACE_PAD, STATE_DEV), LINK),
                pltpu.VMEM((STEPS, 2, COEFS + FACE_PAD, STATE_DEV), LINK),
                pltpu.VMEM((STEPS, 2, COEFS, STATE_DEV), LINK),
                pltpu.VMEM((STEPS, 2, 2, COEFS, STATE_DEV), LINK),
                pltpu.VMEM((5, 128), F32),
                pltpu.VMEM((ns, 5, 128), F32),
                dma((3,)),
                dma((2, 2)),
                dma((STEPS, 2, 2)),
                dma((STEPS, 2, 2)),
                dma((STEPS, 2, 2)),
                dma((2, ns - 1)),
            ],
            compiler_params=pltpu.CompilerParams(collective_id=0, has_side_effects=True),
        )(
            filter_input,
            jnp.swapaxes(cell_table, 0, 1),
            cell_type,
            atom_center,
            proj_values,
            coupling,
            occupation.reshape(1, STATE_DEV),
        )
        return filtered, density

    in_specs = (
        P("cells", "states"),
        P(),
        P("cells"),
        P("cells"),
        P("cells", None, None, None),
        P(),
        P("states"),
    )
    out_specs = (P("cells", "states"), P("cells"))
    return jax.shard_map(body, mesh=mesh, in_specs=in_specs, out_specs=out_specs, check_vma=False)
```

```python
import functools

import jax
import jax.numpy as jnp
from jax import lax
from jax.experimental import pallas as pl
from jax.experimental.pallas import tpu as pltpu
from jax.sharding import PartitionSpec as P

PROJECTORS = 16
STEPS = 3
FACE = 49
CELL_NODES = 343
STRIDE = 294
CELL_DEV = 2
NTYPE = 8
ATOM_DEV = 4
NODE_DEV = 637
STATE_DEV = 128
COEFS = ATOM_DEV * PROJECTORS

lower_edge = 4.0
upper_edge = 12.0
ground_edge = -2.0

DEPTH = 384
ROWS = 352
WIDE_ROWS = 360
FIELD = 688
TAIL = 288
TAIL_SKIP = STRIDE - TAIL
HEAD_ROWS = 344
TAIL_COL = 256
FACE_PAD = 56
SIDE = COEFS - PROJECTORS
NEAR_ROWS = COEFS + FACE_PAD + SIDE

BF = jnp.bfloat16
F32 = jnp.float32
MESH = pl.DeviceIdType.MESH


def mm(a, b):
    return jnp.dot(a, b, preferred_element_type=F32)


def mm_nt(a, b):
    return lax.dot_general(a, b, (((1,), (1,)), ((), ())), preferred_element_type=F32)


def scales():
    half_width = (upper_edge - lower_edge) / 2.0
    scale_now = half_width / (ground_edge - (upper_edge + lower_edge) / 2.0)
    twice_inverse = 2.0 / scale_now
    pairs = [(scale_now / half_width, 0.0)]
    for _ in range(STEPS - 1):
        scale_next = 1.0 / (twice_inverse - scale_now)
        pairs.append((2.0 * scale_next / half_width, scale_now * scale_next))
        scale_now = scale_next
    return pairs


def split(value):
    high = value.astype(BF)
    return high, (value - high.astype(F32)).astype(BF)


def kernel(
    nc,
    ns,
    x_hbm,
    tab_hbm,
    type_hbm,
    center_hbm,
    proj_hbm,
    coup_hbm,
    occ_hbm,
    out_x,
    out_d,
    xin,
    x_left,
    x_right,
    tab,
    types,
    centers,
    proj,
    coup_ref,
    occ_ref,
    hwide,
    hmat,
    hface,
    own,
    own_mixed,
    edge_mixed,
    side_mixed,
    ends_send,
    ends_recv,
    spread_mat,
    face_wide,
    face_mat,
    field,
    near_send,
    near_recv,
    far_recv,
    whole_send,
    whole_recv,
    dens_send,
    dens_recv,
    load_sem,
    raw_sems,
    ends_sems,
    near_sems,
    whole_sems,
    far_sems,
    dens_sems,
    token_sems,
):
    here = lax.axis_index("cells")
    column = lax.axis_index("states")

    def cell_at(shift):
        return {"cells": lax.rem(here + (shift + nc), nc)}

    def state_at(shift):
        return {"states": lax.rem(column + (shift + ns), ns)}

    barrier = pltpu.get_barrier_semaphore()
    for shift in (-1, 1):
        pl.semaphore_signal(barrier, inc=1, device_id=cell_at(shift), device_id_type=MESH)
        pl.semaphore_signal(barrier, inc=1, device_id=state_at(shift), device_id_type=MESH)

    sources = (center_hbm, proj_hbm, x_hbm, coup_hbm, type_hbm, tab_hbm, occ_hbm)
    targets = (centers, proj, xin, coup_ref, types, tab, occ_ref)
    loads = [pltpu.make_async_copy(*pair, load_sem.at[i]) for i, pair in enumerate(zip(sources, targets))]
    for load in loads:
        load.start()

    def send(src, dst, sems, slot, device):
        copy = pltpu.make_async_remote_copy(
            src_ref=src,
            dst_ref=dst,
            send_sem=sems.at[0, slot],
            recv_sem=sems.at[1, slot],
            device_id=device,
            device_id_type=MESH,
        )
        copy.start()
        return copy

    pl.semaphore_wait(barrier, 4)
    raw = [
        send(x_hbm.at[pl.ds(0, HEAD_ROWS)], x_right, raw_sems, 0, cell_at(-1)),
        send(x_hbm.at[pl.ds(TAIL, NODE_DEV - TAIL)], x_left, raw_sems, 1, cell_at(1)),
    ]

    def tell(turn):
        for shift in (-1 - turn, 1 + turn):
            pl.semaphore_signal(token_sems.at[turn], inc=1, device_id=state_at(shift), device_id_type=MESH)

    turns = 2 if ns > 5 else (1 if ns > 3 else 0)
    if turns > 0:
        tell(0)

    own[...] = jnp.zeros_like(own)
    ends_send[...] = jnp.zeros_like(ends_send)

    loads[0].wait()
    loads[1].wait()
    spots = [centers[atom] for atom in range(ATOM_DEV)]
    on_last = sum(spots)
    on_first = ATOM_DEV - on_last
    places = []
    for atom in range(ATOM_DEV):
        ones = sum(spots[:atom]) if atom else 0
        places.append(jnp.where(spots[atom] == 0, atom - ones, on_first + ones))
    for rank in range(ATOM_DEV):
        atom = sum(jnp.where(places[k] == rank, k, 0) for k in range(ATOM_DEV))
        first = rank < on_first
        rows = pl.ds(rank * PROJECTORS, PROJECTORS)
        before, middle, after = (proj[atom, j].astype(F32) for j in range(3))
        zero = jnp.zeros_like(before)
        own[0, rows, :CELL_NODES] = jnp.where(first, middle, before).astype(BF)
        own[1, rows, :CELL_NODES] = jnp.where(first, after, middle).astype(BF)
        if rank < ATOM_DEV - 1:
            ends_send[0, rows, :CELL_NODES] = jnp.where(first, before, zero).astype(BF)
        if rank > 0:
            ends_send[1, rows, :CELL_NODES] = jnp.where(first, zero, after).astype(BF)
    ends_send[0, :, DEPTH:] = own[0, :, :128]
    ends_send[1, :, DEPTH:] = own[1, :, TAIL_COL:]
    ends = [
        send(ends_send.at[0], ends_recv.at[1], ends_sems, 0, cell_at(-1)),
        send(ends_send.at[1], ends_recv.at[0], ends_sems, 1, cell_at(1)),
    ]

    field[:, NODE_DEV - 5 :, :] = jnp.zeros((STEPS, FIELD - NODE_DEV + 5, STATE_DEV), F32)
    hwide[...] = jnp.zeros_like(hwide)
    dens_send[...] = jnp.zeros_like(dens_send)
    loads[2].wait()
    field[0, :NODE_DEV, :] = xin[...].astype(F32)

    loads[3].wait()
    pick = (
        lax.rem(lax.broadcasted_iota(jnp.int32, (COEFS, PROJECTORS), 0), PROJECTORS)
        == lax.broadcasted_iota(jnp.int32, (COEFS, PROJECTORS), 1)
    )
    pick = jnp.where(pick, 1.0, 0.0).astype(BF)
    same = lax.div(lax.broadcasted_iota(jnp.int32, (COEFS, COEFS), 0), PROJECTORS) == lax.div(
        lax.broadcasted_iota(jnp.int32, (COEFS, COEFS), 1), PROJECTORS
    )
    mix_high, mix_low = (
        jnp.where(same, mm_nt(mm(pick, piece).astype(BF), pick), 0.0).astype(BF) for piece in split(coup_ref[...])
    )

    def mixed(rows):
        return mm(mix_high, rows) + mm(mix_low, rows)

    def fold(both):
        half = both.shape[0] // 2
        return both[:half] + both[half:]

    for cell in range(CELL_DEV):
        own_mixed[cell, :COEFS], own_mixed[cell, COEFS:] = split(mixed(own[cell]))
    turned = pltpu.roll(mixed(ends_send[0, :, :DEPTH]), TAIL_SKIP, 1)
    edge_mixed[0, :COEFS], edge_mixed[0, COEFS:] = split(turned)
    edge_mixed[1, :COEFS], edge_mixed[1, COEFS:] = split(mixed(ends_send[1, :, :DEPTH]))

    loads[4].wait()
    loads[5].wait()
    chunk = 256 // NTYPE
    spot = lax.broadcasted_iota(jnp.int32, (CELL_DEV * chunk, 256), 0)
    kind = jnp.where(spot < chunk, types[0], types[1])
    take = lax.broadcasted_iota(jnp.int32, (CELL_DEV * chunk, 256), 1) == lax.rem(spot, chunk) * NTYPE + kind
    take = jnp.where(take, 1.0, 0.0).astype(BF)
    for start in range(0, CELL_NODES, chunk):
        count = min(chunk, CELL_NODES - start)
        entries = tab[start : start + count].reshape(count * NTYPE, CELL_NODES)
        rows = mm(take[:, : count * NTYPE], entries)
        for cell in range(CELL_DEV):
            hwide[cell, start : start + count, :CELL_NODES] = rows[cell * chunk : cell * chunk + count]
    hmat[...] = hwide[:, :ROWS].astype(BF)
    hface[0] = hwide[0, :COEFS].astype(BF)
    hface[1] = hwide[1, STRIDE : STRIDE + COEFS].astype(BF)

    own_part = slice(0, COEFS)
    face_part = slice(COEFS, COEFS + FACE_PAD)
    side_part = slice(COEFS + FACE_PAD, NEAR_ROWS)
    blank = jnp.zeros((PROJECTORS, STATE_DEV), F32)

    def padded(side, slot):
        return jnp.concatenate([side, blank] if slot else [blank, side], axis=0)

    pending = []
    for step, (gain, back) in enumerate(scales()):
        x = field.at[step]
        cells = (x[:DEPTH, :].astype(BF), x[STRIDE : STRIDE + DEPTH, :].astype(BF))

        mine = fold(mm(own_mixed[0], cells[0]) + mm(own_mixed[1], cells[1]))
        copies = []
        sides = []
        for slot, shift in ((0, -1), (1, 1)):
            near_send[step, slot, face_part] = mm(hface[slot], cells[slot])[:FACE_PAD]
            part = face_part
            if step:
                near_send[step, slot, own_part] = mine
                side = fold(mm(side_mixed[slot], cells[slot]))
                near_send[step, slot, side_part] = side
                sides.append(padded(side, slot))
                part = slice(0, NEAR_ROWS)
            rows = pl.ds(part.start, part.stop - part.start)
            copies.append(
                send(
                    near_send.at[step, slot, rows],
                    near_recv.at[step, 1 - slot, rows],
                    near_sems.at[step],
                    slot,
                    cell_at(shift),
                )
            )
            if step:
                copies.append(
                    send(
                        near_send.at[step, slot, pl.ds(side_part.start, SIDE)],
                        far_recv.at[step - 1, 1 - slot],
                        far_sems.at[step - 1],
                        slot,
                        cell_at(2 * shift),
                    )
                )

        if step == 0:
            for copy in raw:
                copy.wait_recv()
            edges = mm(edge_mixed[0, :, : NODE_DEV - TAIL], x_left[...])
            edges = edges + mm(edge_mixed[1, :, :HEAD_ROWS], x_right[...])
            weighted = (mine + fold(edges)).astype(BF)
            whole_send[...] = weighted
            copies += [
                send(whole_send, whole_recv.at[1 - slot], whole_sems, slot, cell_at(shift))
                for slot, shift in ((0, -1), (1, 1))
            ]
        pending += copies

        target = out_x if step == STEPS - 1 else field.at[step + 1]
        centre = (upper_edge + lower_edge) / 2.0
        base = (-centre * gain) * x[:NODE_DEV, :]
        if step:
            base = base - back * field[step - 1, :NODE_DEV, :]
        target[:NODE_DEV, :] = base
        target[:CELL_NODES, :] += gain * mm(hmat[0], cells[0])[:CELL_NODES]
        target[STRIDE:NODE_DEV, :] += gain * mm(hmat[1], cells[1])[:CELL_NODES]

        if step == 0:
            for copy in ends:
                copy.wait_recv()
            for slot in (0, 1):
                side_mixed[slot, :SIDE], side_mixed[slot, SIDE:] = split(
                    mixed(ends_recv[slot, :, :DEPTH])[PROJECTORS * (1 - slot) : PROJECTORS * (1 - slot) + SIDE]
                )
            spread_mat[0] = jnp.concatenate([ends_recv[0, :, :DEPTH], own[0]], axis=0).astype(F32).T.astype(BF)
            spread_mat[1] = jnp.concatenate([own[1], ends_recv[1, :, :DEPTH]], axis=0).astype(F32).T.astype(BF)
            face_wide[0] = jnp.concatenate(
                [ends_recv[0, :, DEPTH:], ends_send[0, :, TAIL_COL:DEPTH]], axis=0
            ).astype(F32).T
            face_wide[1] = jnp.concatenate(
                [ends_send[1, :, :128], ends_recv[1, :, DEPTH:]], axis=0
            ).astype(F32).T
            skip = STRIDE - TAIL_COL
            face_mat[0] = face_wide[0, skip : skip + FACE_PAD, :].astype(BF)
            face_mat[1] = face_wide[1, :FACE_PAD, :].astype(BF)

        for copy in copies:
            copy.wait_recv()
        near = [near_recv.at[step, slot] for slot in (0, 1)]
        if step == 0:
            before, middle, after = whole_recv[0], weighted, whole_recv[1]
        else:
            before = sides[0] + near[0][own_part] + padded(far_recv[step - 1, 0], 1)
            middle = mine + padded(near[0][side_part], 1) + padded(near[1][side_part], 0)
            after = sides[1] + near[1][own_part] + padded(far_recv[step - 1, 1], 0)
            before, middle, after = before.astype(BF), middle.astype(BF), after.astype(BF)
        left = jnp.concatenate([before, middle], axis=0)
        right = jnp.concatenate([middle, after], axis=0)
        face = slice(COEFS, COEFS + FACE)
        target[:CELL_NODES, :] += gain * mm(spread_mat[0], left)[:CELL_NODES]
        target[STRIDE:NODE_DEV, :] += gain * mm(spread_mat[1], right)[:CELL_NODES]
        target[:FACE, :] += gain * (mm(face_mat[0], left)[:FACE] + near[0][face])
        target[NODE_DEV - FACE : NODE_DEV, :] += gain * (mm(face_mat[1], right)[:FACE] + near[1][face])

        if step < turns:
            pl.semaphore_wait(token_sems.at[step], 2)
            if step + 1 < turns:
                tell(step + 1)

    high, low = split(out_x[...] * out_x[...])
    loads[6].wait()
    weight = occ_ref[...] * (1.0 / (STATE_DEV * ns))
    weight_high = weight.astype(BF).astype(F32)
    row = lax.broadcasted_iota(jnp.int32, (16, STATE_DEV), 0)
    weights = jnp.where(row == 0, weight_high, jnp.where(row == 1, weight - weight_high, 0.0)).astype(BF)
    sums = mm_nt(weights, high) + mm_nt(weights, low)
    sums = sums[0:1] + sums[1:2]
    tiles = dens_send.shape[0]
    for tile in range(tiles):
        end = min(NODE_DEV, (tile + 1) * 128)
        dens_send[tile : tile + 1, : end - tile * 128] = sums[:, tile * 128 : end]
    dens_copies = []
    for shift in sorted(range(1, ns), key=lambda k: -min(k, ns - k)):
        dens_copies.append(send(dens_send, dens_recv.at[column], dens_sems, shift - 1, state_at(shift)))
    dens_recv[column] = dens_send[...]
    for copy in raw + ends + pending:
        copy.wait_send()
    for copy in dens_copies:
        copy.wait_recv()
    total = dens_recv[0]
    for peer in range(1, ns):
        total = total + dens_recv[peer]
    for tile in range(tiles):
        end = min(NODE_DEV, (tile + 1) * 128)
        out_d[tile * 128 : end] = total[tile, : end - tile * 128]
    for copy in dens_copies:
        copy.wait_send()


def solution(mesh):
    nc, ns = mesh.shape["cells"], mesh.shape["states"]

    def body(filter_input, cell_table, cell_type, atom_center, proj_values, coupling, occupation):
        any_space = pl.BlockSpec(memory_space=pl.ANY)
        vmem = pl.BlockSpec(memory_space=pltpu.VMEM)
        dma = pltpu.SemaphoreType.DMA
        filtered, density = pl.pallas_call(
            functools.partial(kernel, nc, ns),
            out_shape=(pltpu.VMEM((NODE_DEV, STATE_DEV), F32), pltpu.VMEM((NODE_DEV,), F32)),
            in_specs=[any_space] * 7,
            out_specs=(vmem, vmem),
            scratch_shapes=[
                pltpu.VMEM((NODE_DEV, STATE_DEV), BF),
                pltpu.VMEM((NODE_DEV - TAIL, STATE_DEV), BF),
                pltpu.VMEM((HEAD_ROWS, STATE_DEV), BF),
                pltpu.VMEM((CELL_NODES, NTYPE, CELL_NODES), BF),
                pltpu.SMEM(cell_type.shape, jnp.int32),
                pltpu.SMEM(atom_center.shape, jnp.int32),
                pltpu.VMEM(proj_values.shape, BF),
                pltpu.VMEM(coupling.shape, F32),
                pltpu.VMEM((1, STATE_DEV), F32),
                pltpu.VMEM((CELL_DEV, WIDE_ROWS, DEPTH), F32),
                pltpu.VMEM((CELL_DEV, ROWS, DEPTH), BF),
                pltpu.VMEM((2, COEFS, DEPTH), BF),
                pltpu.VMEM((CELL_DEV, COEFS, DEPTH), BF),
                pltpu.VMEM((CELL_DEV, 2 * COEFS, DEPTH), BF),
                pltpu.VMEM((2, 2 * COEFS, DEPTH), BF),
                pltpu.VMEM((2, 2 * SIDE, DEPTH), BF),
                pltpu.VMEM((2, COEFS, DEPTH + 128), BF),
                pltpu.VMEM((2, COEFS, DEPTH + 128), BF),
                pltpu.VMEM((2, DEPTH, 2 * COEFS), BF),
                pltpu.VMEM((2, 128, 2 * COEFS), F32),
                pltpu.VMEM((2, FACE_PAD, 2 * COEFS), BF),
                pltpu.VMEM((STEPS, FIELD, STATE_DEV), F32),
                pltpu.VMEM((STEPS, 2, NEAR_ROWS, STATE_DEV), F32),
                pltpu.VMEM((STEPS, 2, NEAR_ROWS, STATE_DEV), F32),
                pltpu.VMEM((STEPS - 1, 2, SIDE, STATE_DEV), F32),
                pltpu.VMEM((COEFS, STATE_DEV), BF),
                pltpu.VMEM((2, COEFS, STATE_DEV), BF),
                pltpu.VMEM((5, 128), F32),
                pltpu.VMEM((ns, 5, 128), F32),
                dma((7,)),
                dma((2, 2)),
                dma((2, 2)),
                dma((STEPS, 2, 2)),
                dma((2, 2)),
                dma((STEPS - 1, 2, 2)),
                dma((2, ns - 1)),
                pltpu.SemaphoreType.REGULAR((2,)),
            ],
            compiler_params=pltpu.CompilerParams(collective_id=0, has_side_effects=True),
        )(
            filter_input,
            jnp.swapaxes(cell_table, 0, 1),
            cell_type,
            atom_center,
            proj_values,
            coupling,
            occupation.reshape(1, STATE_DEV),
        )
        return filtered, density

    in_specs = (
        P("cells", "states"),
        P(),
        P("cells"),
        P("cells"),
        P("cells", None, None, None),
        P(),
        P("states"),
    )
    out_specs = (P("cells", "states"), P("cells"))
    return jax.shard_map(body, mesh=mesh, in_specs=in_specs, out_specs=out_specs, check_vma=False)
```

```python
import functools

import jax
import jax.numpy as jnp
from jax import lax
from jax.experimental import pallas as pl
from jax.experimental.pallas import tpu as pltpu
from jax.sharding import PartitionSpec as P

PROJECTORS = 16
STEPS = 3
FACE = 49
CELL_NODES = 343
STRIDE = 294
CELL_DEV = 2
NTYPE = 8
ATOM_DEV = 4
NODE_DEV = 637
STATE_DEV = 128
COEFS = ATOM_DEV * PROJECTORS

lower_edge = 4.0
upper_edge = 12.0
ground_edge = -2.0

DEPTH = 384
ROWS = 352
WIDE_ROWS = 368
BLOCK = 640
FIELD = 672
TAIL = 288
TAIL_SKIP = STRIDE - TAIL
HEAD_ROWS = 344
TAIL_COL = 256
FACE_PAD = 56
LAST_SKIP = NODE_DEV - FACE - (BLOCK - FACE_PAD)
SIDE = COEFS - PROJECTORS
NEAR_ROWS = COEFS + FACE_PAD + SIDE

BF = jnp.bfloat16
F32 = jnp.float32
MESH = pl.DeviceIdType.MESH


def mm(a, b):
    return jnp.dot(a, b, preferred_element_type=F32)


def mm_nt(a, b):
    return lax.dot_general(a, b, (((1,), (1,)), ((), ())), preferred_element_type=F32)


def scales():
    half_width = (upper_edge - lower_edge) / 2.0
    scale_now = half_width / (ground_edge - (upper_edge + lower_edge) / 2.0)
    twice_inverse = 2.0 / scale_now
    pairs = [(scale_now / half_width, 0.0)]
    for _ in range(STEPS - 1):
        scale_next = 1.0 / (twice_inverse - scale_now)
        pairs.append((2.0 * scale_next / half_width, scale_now * scale_next))
        scale_now = scale_next
    return pairs


def split(value):
    high = value.astype(BF)
    return high, (value - high.astype(F32)).astype(BF)


def kernel(
    nc,
    ns,
    x_hbm,
    tab_hbm,
    type_hbm,
    center_hbm,
    proj_hbm,
    coup_hbm,
    occ_hbm,
    out_x,
    out_d,
    xin,
    x_left,
    x_right,
    tab,
    types,
    centers,
    proj,
    coup_ref,
    occ_ref,
    hwide,
    hmat,
    own,
    probe,
    edge_mixed,
    ends_send,
    ends_recv,
    spread_wide,
    spread_mat,
    face_wide,
    face_mat,
    field,
    base_ref,
    near_send,
    near_recv,
    far_recv,
    whole_send,
    whole_recv,
    dens_send,
    dens_recv,
    load_sem,
    raw_sems,
    ends_sems,
    near_sems,
    whole_sems,
    far_sems,
    side_sems,
    own_sems,
    dens_sems,
    token_sems,
):
    here = lax.axis_index("cells")
    column = lax.axis_index("states")

    def cell_at(shift):
        return {"cells": lax.rem(here + (shift + nc), nc)}

    def state_at(shift):
        return {"states": lax.rem(column + (shift + ns), ns)}

    barrier = pltpu.get_barrier_semaphore()
    for shift in (-1, 1):
        pl.semaphore_signal(barrier, inc=1, device_id=cell_at(shift), device_id_type=MESH)
        pl.semaphore_signal(barrier, inc=1, device_id=state_at(shift), device_id_type=MESH)

    sources = (center_hbm, proj_hbm, x_hbm, coup_hbm, type_hbm, tab_hbm, occ_hbm)
    targets = (centers, proj, xin, coup_ref, types, tab, occ_ref)
    loads = [pltpu.make_async_copy(*pair, load_sem.at[i]) for i, pair in enumerate(zip(sources, targets))]
    for load in loads:
        load.start()

    def send(src, dst, sems, slot, device):
        copy = pltpu.make_async_remote_copy(
            src_ref=src,
            dst_ref=dst,
            send_sem=sems.at[0, slot],
            recv_sem=sems.at[1, slot],
            device_id=device,
            device_id_type=MESH,
        )
        copy.start()
        return copy

    pl.semaphore_wait(barrier, 4)
    raw = [
        send(x_hbm.at[pl.ds(0, HEAD_ROWS)], x_right, raw_sems, 0, cell_at(-1)),
        send(x_hbm.at[pl.ds(TAIL, NODE_DEV - TAIL)], x_left, raw_sems, 1, cell_at(1)),
    ]

    def tell(turn):
        for shift in (-1 - turn, 1 + turn):
            pl.semaphore_signal(token_sems.at[turn], inc=1, device_id=state_at(shift), device_id_type=MESH)

    turns = 2 if ns > 5 else (1 if ns > 3 else 0)
    if turns > 0:
        tell(0)

    own[...] = jnp.zeros_like(own)
    ends_send[...] = jnp.zeros_like(ends_send)

    loads[0].wait()
    loads[1].wait()
    spots = [centers[atom] for atom in range(ATOM_DEV)]
    on_last = sum(spots)
    on_first = ATOM_DEV - on_last
    places = []
    for atom in range(ATOM_DEV):
        ones = sum(spots[:atom]) if atom else 0
        places.append(jnp.where(spots[atom] == 0, atom - ones, on_first + ones))
    for rank in range(ATOM_DEV):
        atom = sum(jnp.where(places[k] == rank, k, 0) for k in range(ATOM_DEV))
        first = rank < on_first
        rows = pl.ds(rank * PROJECTORS, PROJECTORS)
        before, middle, after = (proj[atom, j].astype(F32) for j in range(3))
        zero = jnp.zeros_like(before)
        own[0, rows, :CELL_NODES] = jnp.where(first, middle, before).astype(BF)
        own[1, rows, :CELL_NODES] = jnp.where(first, after, middle).astype(BF)
        if rank < ATOM_DEV - 1:
            ends_send[0, rows, :CELL_NODES] = jnp.where(first, before, zero).astype(BF)
        if rank > 0:
            ends_send[1, rows, :CELL_NODES] = jnp.where(first, zero, after).astype(BF)
    ends_send[0, :, DEPTH:] = own[0, :, :128]
    ends_send[1, :, DEPTH:] = own[1, :, TAIL_COL:]
    ends = [
        send(ends_send.at[0], ends_recv.at[1], ends_sems, 0, cell_at(-1)),
        send(ends_send.at[1], ends_recv.at[0], ends_sems, 1, cell_at(1)),
    ]

    field[:, NODE_DEV - 5 :, :] = jnp.zeros((STEPS, FIELD - NODE_DEV + 5, STATE_DEV), F32)
    hwide[...] = jnp.zeros_like(hwide)
    spread_wide[...] = jnp.zeros_like(spread_wide)
    face_wide[...] = jnp.zeros_like(face_wide)
    dens_send[...] = jnp.zeros_like(dens_send)
    loads[2].wait()
    field[0, :NODE_DEV, :] = xin[...].astype(F32)

    loads[3].wait()
    pick = (
        lax.rem(lax.broadcasted_iota(jnp.int32, (COEFS, PROJECTORS), 0), PROJECTORS)
        == lax.broadcasted_iota(jnp.int32, (COEFS, PROJECTORS), 1)
    )
    pick = jnp.where(pick, 1.0, 0.0).astype(BF)
    same = lax.div(lax.broadcasted_iota(jnp.int32, (COEFS, COEFS), 0), PROJECTORS) == lax.div(
        lax.broadcasted_iota(jnp.int32, (COEFS, COEFS), 1), PROJECTORS
    )
    mix_high, mix_low = (
        jnp.where(same, mm_nt(mm(pick, piece).astype(BF), pick), 0.0).astype(BF) for piece in split(coup_ref[...])
    )

    def mixed(rows):
        return mm(mix_high, rows) + mm(mix_low, rows)

    def fold(both):
        half = both.shape[0] // 2
        return both[:half] + both[half:]

    def moved(value, cell):
        return pltpu.roll(value, TAIL_SKIP, 1) if cell else value

    for cell in range(CELL_DEV):
        probe[cell, :COEFS], probe[cell, COEFS : 2 * COEFS] = split(moved(mixed(own[cell]), cell))
        edge_mixed[cell, :COEFS], edge_mixed[cell, COEFS:] = split(
            moved(mixed(ends_send[cell, :, :DEPTH]), 1 - cell)
        )

    faces = slice(2 * COEFS, 3 * COEFS)
    loads[4].wait()
    loads[5].wait()
    chunk = 256 // NTYPE
    spot = lax.broadcasted_iota(jnp.int32, (CELL_DEV * chunk, 256), 0)
    kind = jnp.where(spot < chunk, types[0], types[1])
    take = lax.broadcasted_iota(jnp.int32, (CELL_DEV * chunk, 256), 1) == lax.rem(spot, chunk) * NTYPE + kind
    take = jnp.where(take, 1.0, 0.0).astype(BF)
    for start in range(0, CELL_NODES, chunk):
        count = min(chunk, CELL_NODES - start)
        entries = tab[start : start + count].reshape(count * NTYPE, CELL_NODES)
        rows = mm(take[:, : count * NTYPE], entries)
        for cell in range(CELL_DEV):
            begin = start + cell * TAIL_SKIP
            hwide[cell, begin : begin + count, :CELL_NODES] = rows[cell * chunk : cell * chunk + count]
    hwide[1] = moved(hwide[1], 1)
    hmat[...] = hwide[:, :ROWS].astype(BF)
    probe[1, faces] = hwide[1, STRIDE + TAIL_SKIP : STRIDE + TAIL_SKIP + COEFS].astype(BF)
    hwide[0, LAST_SKIP : LAST_SKIP + FACE] = hwide[0, :FACE]
    hwide[0, :LAST_SKIP] = jnp.zeros((LAST_SKIP, DEPTH), F32)
    hwide[0, LAST_SKIP + FACE : COEFS] = jnp.zeros((COEFS - LAST_SKIP - FACE, DEPTH), F32)
    probe[0, faces] = hwide[0, :COEFS].astype(BF)

    own_part = slice(0, COEFS)
    face_part = slice(COEFS, COEFS + FACE_PAD)
    side_part = slice(COEFS + FACE_PAD, NEAR_ROWS)
    blank = jnp.zeros((PROJECTORS, STATE_DEV), F32)

    def padded(side, slot):
        return jnp.concatenate([side, blank] if slot else [blank, side], axis=0)

    pending = []
    for step, (gain, back) in enumerate(scales()):
        x = field.at[step]
        rounded = x[...].astype(BF)
        cells = (rounded[:DEPTH], rounded[TAIL:])
        copies = []
        sides = []

        def exchange(part, sems):
            rows = pl.ds(part.start, part.stop - part.start)
            for slot, shift in ((0, -1), (1, 1)):
                copies.append(
                    send(
                        near_send.at[step, slot, rows],
                        near_recv.at[step, 1 - slot, rows],
                        sems,
                        slot,
                        cell_at(shift),
                    )
                )

        if step:
            for slot, shift in ((0, -1), (1, 1)):
                side = fold(mm(probe[slot, 3 * COEFS :], cells[slot]))
                near_send[step, slot, side_part] = side
                sides.append(padded(side, slot))
                copies.append(
                    send(
                        near_send.at[step, slot, pl.ds(side_part.start, SIDE)],
                        far_recv.at[step - 1, 1 - slot],
                        far_sems.at[step - 1],
                        slot,
                        cell_at(2 * shift),
                    )
                )
            exchange(side_part, side_sems.at[step - 1])
        mine = fold(mm(probe[0, : 2 * COEFS], cells[0]) + mm(probe[1, : 2 * COEFS], cells[1]))
        if step:
            for slot in (0, 1):
                near_send[step, slot, own_part] = mine
            exchange(own_part, own_sems.at[step - 1])
        for slot in (0, 1):
            near_send[step, slot, face_part] = mm(probe[slot, faces], cells[slot])[:FACE_PAD]
        exchange(face_part, near_sems.at[step])

        if step == 0:
            for copy in raw:
                copy.wait_recv()
            edges = mm(edge_mixed[0, :, : NODE_DEV - TAIL], x_left[...])
            edges = edges + mm(edge_mixed[1, :, :HEAD_ROWS], x_right[...])
            weighted = (mine + fold(edges)).astype(BF)
            whole_send[...] = weighted
            copies += [
                send(whole_send, whole_recv.at[1 - slot], whole_sems, slot, cell_at(shift))
                for slot, shift in ((0, -1), (1, 1))
            ]
        pending += copies

        centre = (upper_edge + lower_edge) / 2.0
        base = (-centre * gain) * x[:BLOCK, :]
        if step:
            base = base - back * field[step - 1, :BLOCK, :]
        base_ref[...] = base
        base_ref[:ROWS, :] += gain * mm(hmat[0], cells[0])
        base_ref[TAIL:, :] += gain * mm(hmat[1], cells[1])

        if step == 0:
            for copy in ends:
                copy.wait_recv()
            for slot in (0, 1):
                skip = PROJECTORS * (1 - slot)
                side = moved(mixed(ends_recv[slot, :, :DEPTH])[skip : skip + SIDE], slot)
                probe[slot, 3 * COEFS : 3 * COEFS + SIDE], probe[slot, 3 * COEFS + SIDE :] = split(side)
            spread_wide[:DEPTH, : 2 * COEFS] = (
                jnp.concatenate([ends_recv[0, :, :DEPTH], own[0]], axis=0).astype(F32).T
            )
            spread_wide[STRIDE : STRIDE + DEPTH, 2 * COEFS :] = (
                jnp.concatenate([own[1], ends_recv[1, :, :DEPTH]], axis=0).astype(F32).T
            )
            spread_mat[...] = spread_wide[:BLOCK].astype(BF)
            skip = STRIDE - TAIL_COL
            face_wide[0, :128] = (
                jnp.concatenate([ends_recv[0, :, DEPTH:], ends_send[0, :, TAIL_COL:DEPTH]], axis=0).astype(F32).T
            )
            ahead = jnp.concatenate([ends_send[1, :, :128], ends_recv[1, :, DEPTH:]], axis=0).astype(F32).T
            face_wide[1, LAST_SKIP : LAST_SKIP + FACE] = ahead[:FACE]
            face_mat[0] = face_wide[0, skip : skip + COEFS].astype(BF)
            face_mat[1] = face_wide[1, :COEFS].astype(BF)

        for copy in copies:
            copy.wait_recv()
        near = [near_recv.at[step, slot] for slot in (0, 1)]
        if step == 0:
            before, middle, after = whole_recv[0], weighted, whole_recv[1]
        else:
            before = sides[0] + near[0][own_part] + padded(far_recv[step - 1, 0], 1)
            middle = mine + padded(near[0][side_part], 1) + padded(near[1][side_part], 0)
            after = sides[1] + near[1][own_part] + padded(far_recv[step - 1, 1], 0)
            before, middle, after = before.astype(BF), middle.astype(BF), after.astype(BF)
        left = jnp.concatenate([before, middle], axis=0)
        right = jnp.concatenate([middle, after], axis=0)
        both = jnp.concatenate([left, right], axis=0)
        half = BLOCK // 2
        spread = jnp.concatenate([mm(spread_mat[:half], both), mm(spread_mat[half:], both)], axis=0)
        top = mm(face_mat[0], left)[:FACE_PAD] + near[0][face_part]
        bottom = mm(face_mat[1], right)[:FACE_PAD] + near[1][face_part]
        spread = jnp.concatenate(
            [
                spread[:FACE_PAD] + top,
                spread[FACE_PAD : BLOCK - FACE_PAD],
                spread[BLOCK - FACE_PAD :] + bottom,
            ],
            axis=0,
        )
        following = base_ref[...] + gain * spread
        if step < STEPS - 1:
            field[step + 1, :BLOCK, :] = following
        else:
            out_x[...] = following[:NODE_DEV]

        if step < turns:
            pl.semaphore_wait(token_sems.at[step], 2)
            if step + 1 < turns:
                tell(step + 1)

    high, low = split(following * following)
    loads[6].wait()
    weight = occ_ref[...] * (1.0 / (STATE_DEV * ns))
    weight_high = weight.astype(BF).astype(F32)
    row = lax.broadcasted_iota(jnp.int32, (16, STATE_DEV), 0)
    weights = jnp.where(row == 0, weight_high, jnp.where(row == 1, weight - weight_high, 0.0)).astype(BF)
    sums = mm_nt(weights, high) + mm_nt(weights, low)
    sums = sums[0:1] + sums[1:2]
    tiles = dens_send.shape[0]
    for tile in range(tiles):
        end = min(NODE_DEV, (tile + 1) * 128)
        dens_send[tile : tile + 1, : end - tile * 128] = sums[:, tile * 128 : end]
    dens_copies = []
    for shift in sorted(range(1, ns), key=lambda k: -min(k, ns - k)):
        dens_copies.append(send(dens_send, dens_recv.at[column], dens_sems, shift - 1, state_at(shift)))
    dens_recv[column] = dens_send[...]
    for copy in raw + ends + pending:
        copy.wait_send()
    for copy in dens_copies:
        copy.wait_recv()
    total = dens_recv[0]
    for peer in range(1, ns):
        total = total + dens_recv[peer]
    for tile in range(tiles):
        end = min(NODE_DEV, (tile + 1) * 128)
        out_d[tile * 128 : end] = total[tile, : end - tile * 128]
    for copy in dens_copies:
        copy.wait_send()


def store(x_ref, d_ref, x_hbm, d_hbm, sem):
    copies = [
        pltpu.make_async_copy(x_ref, x_hbm, sem.at[0]),
        pltpu.make_async_copy(d_ref, d_hbm, sem.at[1]),
    ]
    for copy in copies:
        copy.start()
    for copy in copies:
        copy.wait()


def solution(mesh):
    nc, ns = mesh.shape["cells"], mesh.shape["states"]

    def body(filter_input, cell_table, cell_type, atom_center, proj_values, coupling, occupation):
        any_space = pl.BlockSpec(memory_space=pl.ANY)
        vmem = pl.BlockSpec(memory_space=pltpu.VMEM)
        dma = pltpu.SemaphoreType.DMA
        filtered, density = pl.pallas_call(
            functools.partial(kernel, nc, ns),
            out_shape=(pltpu.VMEM((NODE_DEV, STATE_DEV), F32), pltpu.VMEM((NODE_DEV,), F32)),
            in_specs=[any_space] * 7,
            out_specs=(vmem, vmem),
            scratch_shapes=[
                pltpu.VMEM((NODE_DEV, STATE_DEV), BF),
                pltpu.VMEM((NODE_DEV - TAIL, STATE_DEV), BF),
                pltpu.VMEM((HEAD_ROWS, STATE_DEV), BF),
                pltpu.VMEM((CELL_NODES, NTYPE, CELL_NODES), BF),
                pltpu.SMEM(cell_type.shape, jnp.int32),
                pltpu.SMEM(atom_center.shape, jnp.int32),
                pltpu.VMEM(proj_values.shape, BF),
                pltpu.VMEM(coupling.shape, F32),
                pltpu.VMEM((1, STATE_DEV), F32),
                pltpu.VMEM((CELL_DEV, WIDE_ROWS, DEPTH), F32),
                pltpu.VMEM((CELL_DEV, ROWS, DEPTH), BF),
                pltpu.VMEM((CELL_DEV, COEFS, DEPTH), BF),
                pltpu.VMEM((CELL_DEV, 3 * COEFS + 2 * SIDE, DEPTH), BF),
                pltpu.VMEM((2, 2 * COEFS, DEPTH), BF),
                pltpu.VMEM((2, COEFS, DEPTH + 128), BF),
                pltpu.VMEM((2, COEFS, DEPTH + 128), BF),
                pltpu.VMEM((STRIDE + DEPTH + 2, 4 * COEFS), F32),
                pltpu.VMEM((BLOCK, 4 * COEFS), BF),
                pltpu.VMEM((2, 128, 2 * COEFS), F32),
                pltpu.VMEM((2, COEFS, 2 * COEFS), BF),
                pltpu.VMEM((STEPS, FIELD, STATE_DEV), F32),
                pltpu.VMEM((BLOCK, STATE_DEV), F32),
                pltpu.VMEM((STEPS, 2, NEAR_ROWS, STATE_DEV), F32),
                pltpu.VMEM((STEPS, 2, NEAR_ROWS, STATE_DEV), F32),
                pltpu.VMEM((STEPS - 1, 2, SIDE, STATE_DEV), F32),
                pltpu.VMEM((COEFS, STATE_DEV), BF),
                pltpu.VMEM((2, COEFS, STATE_DEV), BF),
                pltpu.VMEM((5, 128), F32),
                pltpu.VMEM((ns, 5, 128), F32),
                dma((7,)),
                dma((2, 2)),
                dma((2, 2)),
                dma((STEPS, 2, 2)),
                dma((2, 2)),
                dma((STEPS - 1, 2, 2)),
                dma((STEPS - 1, 2, 2)),
                dma((STEPS - 1, 2, 2)),
                dma((2, ns - 1)),
                pltpu.SemaphoreType.REGULAR((2,)),
            ],
            compiler_params=pltpu.CompilerParams(collective_id=0, has_side_effects=True),
        )(
            filter_input,
            jnp.swapaxes(cell_table, 0, 1),
            cell_type,
            atom_center,
            proj_values,
            coupling,
            occupation.reshape(1, STATE_DEV),
        )
        return pl.pallas_call(
            store,
            out_shape=(
                jax.ShapeDtypeStruct((NODE_DEV, STATE_DEV), F32),
                jax.ShapeDtypeStruct((NODE_DEV,), F32),
            ),
            in_specs=[any_space, any_space],
            out_specs=(any_space, any_space),
            scratch_shapes=[dma((2,))],
        )(*(pltpu.with_memory_space_constraint(v, pltpu.VMEM) for v in (filtered, density)))

    in_specs = (
        P("cells", "states"),
        P(),
        P("cells"),
        P("cells"),
        P("cells", None, None, None),
        P(),
        P("states"),
    )
    out_specs = (P("cells", "states"), P("cells"))
    return jax.shard_map(body, mesh=mesh, in_specs=in_specs, out_specs=out_specs, check_vma=False)
```

```python
import functools

import jax
import jax.numpy as jnp
from jax import lax
from jax.experimental import pallas as pl
from jax.experimental.pallas import tpu as pltpu
from jax.sharding import PartitionSpec as P

PROJECTORS = 16
STEPS = 3
FACE = 49
CELL_NODES = 343
STRIDE = 294
CELL_DEV = 2
NTYPE = 8
ATOM_DEV = 4
NODE_DEV = 637
STATE_DEV = 128
COEFS = ATOM_DEV * PROJECTORS

lower_edge = 4.0
upper_edge = 12.0
ground_edge = -2.0

DEPTH = 384
ROWS = 352
WIDE_ROWS = 368
BLOCK = 640
FIELD = 672
TAIL = 288
TAIL_SKIP = STRIDE - TAIL
HEAD_ROWS = 344
TAIL_COL = 256
FACE_PAD = 56
LAST_SKIP = NODE_DEV - FACE - (BLOCK - FACE_PAD)
SIDE = COEFS - PROJECTORS
NEAR_ROWS = COEFS + FACE_PAD + SIDE

BF = jnp.bfloat16
F32 = jnp.float32
MESH = pl.DeviceIdType.MESH


def mm(a, b):
    return jnp.dot(a, b, preferred_element_type=F32)


def mm_nt(a, b):
    return lax.dot_general(a, b, (((1,), (1,)), ((), ())), preferred_element_type=F32)


def scales():
    half_width = (upper_edge - lower_edge) / 2.0
    scale_now = half_width / (ground_edge - (upper_edge + lower_edge) / 2.0)
    twice_inverse = 2.0 / scale_now
    pairs = [(scale_now / half_width, 0.0)]
    for _ in range(STEPS - 1):
        scale_next = 1.0 / (twice_inverse - scale_now)
        pairs.append((2.0 * scale_next / half_width, scale_now * scale_next))
        scale_now = scale_next
    return pairs


def split(value):
    high = value.astype(BF)
    return high, (value - high.astype(F32)).astype(BF)


def kernel(
    nc,
    ns,
    x_hbm,
    tab_hbm,
    type_hbm,
    center_hbm,
    proj_hbm,
    coup_hbm,
    occ_hbm,
    out_x,
    out_d,
    xin,
    x_left,
    x_right,
    tab,
    types,
    centers,
    proj,
    coup_ref,
    occ_ref,
    hwide,
    hmat,
    own,
    probe,
    edge_mixed,
    ends_send,
    ends_recv,
    spread_wide,
    spread_mat,
    face_wide,
    face_mat,
    field,
    base_ref,
    near_send,
    near_recv,
    far_recv,
    whole_send,
    whole_recv,
    dens_send,
    dens_recv,
    load_sem,
    raw_sems,
    ends_sems,
    near_sems,
    whole_sems,
    far_sems,
    side_sems,
    own_sems,
    dens_sems,
    token_sems,
):
    here = lax.axis_index("cells")
    column = lax.axis_index("states")

    def cell_at(shift):
        return {"cells": lax.rem(here + (shift + nc), nc)}

    def state_at(shift):
        return {"states": lax.rem(column + (shift + ns), ns)}

    barrier = pltpu.get_barrier_semaphore()
    for shift in (-1, 1):
        pl.semaphore_signal(barrier, inc=1, device_id=cell_at(shift), device_id_type=MESH)
        pl.semaphore_signal(barrier, inc=1, device_id=state_at(shift), device_id_type=MESH)

    sources = (center_hbm, proj_hbm, x_hbm, coup_hbm, type_hbm, tab_hbm, occ_hbm)
    targets = (centers, proj, xin, coup_ref, types, tab, occ_ref)
    loads = [pltpu.make_async_copy(*pair, load_sem.at[i]) for i, pair in enumerate(zip(sources, targets))]
    for load in loads:
        load.start()

    def send(src, dst, sems, slot, device):
        copy = pltpu.make_async_remote_copy(
            src_ref=src,
            dst_ref=dst,
            send_sem=sems.at[0, slot],
            recv_sem=sems.at[1, slot],
            device_id=device,
            device_id_type=MESH,
        )
        copy.start()
        return copy

    pl.semaphore_wait(barrier, 4)
    raw = [
        send(x_hbm.at[pl.ds(0, HEAD_ROWS)], x_right, raw_sems, 0, cell_at(-1)),
        send(x_hbm.at[pl.ds(TAIL, NODE_DEV - TAIL)], x_left, raw_sems, 1, cell_at(1)),
    ]

    def tell(turn):
        for shift in (-1 - turn, 1 + turn):
            pl.semaphore_signal(token_sems.at[turn], inc=1, device_id=state_at(shift), device_id_type=MESH)

    turns = 2 if ns > 5 else (1 if ns > 3 else 0)
    if turns > 0:
        tell(0)

    own[...] = jnp.zeros_like(own)
    ends_send[...] = jnp.zeros_like(ends_send)

    loads[0].wait()
    loads[1].wait()
    spots = [centers[atom] for atom in range(ATOM_DEV)]
    on_last = sum(spots)
    on_first = ATOM_DEV - on_last
    places = []
    for atom in range(ATOM_DEV):
        ones = sum(spots[:atom]) if atom else 0
        places.append(jnp.where(spots[atom] == 0, atom - ones, on_first + ones))
    for rank in range(ATOM_DEV):
        atom = sum(jnp.where(places[k] == rank, k, 0) for k in range(ATOM_DEV))
        first = rank < on_first
        rows = pl.ds(rank * PROJECTORS, PROJECTORS)
        before, middle, after = (proj[atom, j].astype(F32) for j in range(3))
        zero = jnp.zeros_like(before)
        own[0, rows, :CELL_NODES] = jnp.where(first, middle, before).astype(BF)
        own[1, rows, :CELL_NODES] = jnp.where(first, after, middle).astype(BF)
        if rank < ATOM_DEV - 1:
            ends_send[0, rows, :CELL_NODES] = jnp.where(first, before, zero).astype(BF)
        if rank > 0:
            ends_send[1, rows, :CELL_NODES] = jnp.where(first, zero, after).astype(BF)
    ends_send[0, :, DEPTH:] = own[0, :, :128]
    ends_send[1, :, DEPTH:] = own[1, :, TAIL_COL:]
    ends = [
        send(ends_send.at[0], ends_recv.at[1], ends_sems, 0, cell_at(-1)),
        send(ends_send.at[1], ends_recv.at[0], ends_sems, 1, cell_at(1)),
    ]

    field[:, NODE_DEV - 5 :, :] = jnp.zeros((STEPS, FIELD - NODE_DEV + 5, STATE_DEV), F32)
    hwide[...] = jnp.zeros_like(hwide)
    spread_wide[...] = jnp.zeros_like(spread_wide)
    face_wide[...] = jnp.zeros_like(face_wide)
    dens_send[...] = jnp.zeros_like(dens_send)
    loads[2].wait()
    field[0, :NODE_DEV, :] = xin[...].astype(F32)

    loads[3].wait()
    pick = (
        lax.rem(lax.broadcasted_iota(jnp.int32, (COEFS, PROJECTORS), 0), PROJECTORS)
        == lax.broadcasted_iota(jnp.int32, (COEFS, PROJECTORS), 1)
    )
    pick = jnp.where(pick, 1.0, 0.0).astype(BF)
    same = lax.div(lax.broadcasted_iota(jnp.int32, (COEFS, COEFS), 0), PROJECTORS) == lax.div(
        lax.broadcasted_iota(jnp.int32, (COEFS, COEFS), 1), PROJECTORS
    )
    mix_high, mix_low = (
        jnp.where(same, mm_nt(mm(pick, piece).astype(BF), pick), 0.0).astype(BF) for piece in split(coup_ref[...])
    )

    def mixed(rows):
        return mm(mix_high, rows) + mm(mix_low, rows)

    def fold(both):
        half = both.shape[0] // 2
        return both[:half] + both[half:]

    def moved(value, cell):
        return pltpu.roll(value, TAIL_SKIP, 1) if cell else value

    for cell in range(CELL_DEV):
        probe[cell, :COEFS], probe[cell, COEFS : 2 * COEFS] = split(moved(mixed(own[cell]), cell))
        edge_mixed[cell, :COEFS], edge_mixed[cell, COEFS:] = split(
            moved(mixed(ends_send[cell, :, :DEPTH]), 1 - cell)
        )

    faces = slice(2 * COEFS, 3 * COEFS)
    loads[4].wait()
    loads[5].wait()
    chunk = 256 // NTYPE
    spot = lax.broadcasted_iota(jnp.int32, (CELL_DEV * chunk, 256), 0)
    kind = jnp.where(spot < chunk, types[0], types[1])
    take = lax.broadcasted_iota(jnp.int32, (CELL_DEV * chunk, 256), 1) == lax.rem(spot, chunk) * NTYPE + kind
    take = jnp.where(take, 1.0, 0.0).astype(BF)
    for start in range(0, CELL_NODES, chunk):
        count = min(chunk, CELL_NODES - start)
        entries = tab[start : start + count].reshape(count * NTYPE, CELL_NODES)
        rows = mm(take[:, : count * NTYPE], entries)
        for cell in range(CELL_DEV):
            begin = start + cell * TAIL_SKIP
            hwide[cell, begin : begin + count, :CELL_NODES] = rows[cell * chunk : cell * chunk + count]
    hwide[1] = moved(hwide[1], 1)
    hmat[...] = hwide[:, :ROWS].astype(BF)
    probe[1, faces] = hwide[1, STRIDE + TAIL_SKIP : STRIDE + TAIL_SKIP + COEFS].astype(BF)
    hwide[0, LAST_SKIP : LAST_SKIP + FACE] = hwide[0, :FACE]
    hwide[0, :LAST_SKIP] = jnp.zeros((LAST_SKIP, DEPTH), F32)
    hwide[0, LAST_SKIP + FACE : COEFS] = jnp.zeros((COEFS - LAST_SKIP - FACE, DEPTH), F32)
    probe[0, faces] = hwide[0, :COEFS].astype(BF)

    own_part = slice(0, COEFS)
    face_part = slice(COEFS, COEFS + FACE_PAD)
    side_part = slice(COEFS + FACE_PAD, NEAR_ROWS)
    blank = jnp.zeros((PROJECTORS, STATE_DEV), F32)

    def padded(side, slot):
        return jnp.concatenate([side, blank] if slot else [blank, side], axis=0)

    pending = []
    rounded = field[0].astype(BF)
    for step, (gain, back) in enumerate(scales()):
        x = field.at[step]
        cells = (rounded[:DEPTH], rounded[TAIL:])
        copies = []
        sides = []

        def exchange(part, sems):
            rows = pl.ds(part.start, part.stop - part.start)
            for slot, shift in ((0, -1), (1, 1)):
                copies.append(
                    send(
                        near_send.at[step, slot, rows],
                        near_recv.at[step, 1 - slot, rows],
                        sems,
                        slot,
                        cell_at(shift),
                    )
                )

        mine = fold(mm(probe[0, : 2 * COEFS], cells[0]) + mm(probe[1, : 2 * COEFS], cells[1]))
        if step:
            for slot in (0, 1):
                near_send[step, slot, own_part] = mine
            exchange(own_part, own_sems.at[step - 1])
            for slot, shift in ((0, -1), (1, 1)):
                side = fold(mm(probe[slot, 3 * COEFS :], cells[slot]))
                near_send[step, slot, side_part] = side
                sides.append(padded(side, slot))
                copies.append(
                    send(
                        near_send.at[step, slot, pl.ds(side_part.start, SIDE)],
                        far_recv.at[step - 1, 1 - slot],
                        far_sems.at[step - 1],
                        slot,
                        cell_at(2 * shift),
                    )
                )
            exchange(side_part, side_sems.at[step - 1])
        for slot in (0, 1):
            near_send[step, slot, face_part] = mm(probe[slot, faces], cells[slot])[:FACE_PAD]
        exchange(face_part, near_sems.at[step])

        if step == 0:
            for copy in raw:
                copy.wait_recv()
            edges = mm(edge_mixed[0, :, : NODE_DEV - TAIL], x_left[...])
            edges = edges + mm(edge_mixed[1, :, :HEAD_ROWS], x_right[...])
            weighted = (mine + fold(edges)).astype(BF)
            whole_send[...] = weighted
            copies += [
                send(whole_send, whole_recv.at[1 - slot], whole_sems, slot, cell_at(shift))
                for slot, shift in ((0, -1), (1, 1))
            ]
        pending += copies
        if step == 1 and turns > 0:
            pl.semaphore_wait(token_sems.at[0], 2)
            if turns > 1:
                tell(1)

        centre = (upper_edge + lower_edge) / 2.0
        base = (-centre * gain) * x[:BLOCK, :]
        if step:
            base = base - back * field[step - 1, :BLOCK, :]
        base_ref[...] = base
        base_ref[:ROWS, :] += gain * mm(hmat[0], cells[0])
        base_ref[TAIL:, :] += gain * mm(hmat[1], cells[1])

        if step == 0:
            for copy in ends:
                copy.wait_recv()
            for slot in (0, 1):
                skip = PROJECTORS * (1 - slot)
                side = moved(mixed(ends_recv[slot, :, :DEPTH])[skip : skip + SIDE], slot)
                probe[slot, 3 * COEFS : 3 * COEFS + SIDE], probe[slot, 3 * COEFS + SIDE :] = split(side)
            spread_wide[:DEPTH, : 2 * COEFS] = (
                jnp.concatenate([ends_recv[0, :, :DEPTH], own[0]], axis=0).astype(F32).T
            )
            spread_wide[STRIDE : STRIDE + DEPTH, 2 * COEFS :] = (
                jnp.concatenate([own[1], ends_recv[1, :, :DEPTH]], axis=0).astype(F32).T
            )
            spread_mat[...] = spread_wide[:BLOCK].astype(BF)
            skip = STRIDE - TAIL_COL
            face_wide[0, :128] = (
                jnp.concatenate([ends_recv[0, :, DEPTH:], ends_send[0, :, TAIL_COL:DEPTH]], axis=0).astype(F32).T
            )
            ahead = jnp.concatenate([ends_send[1, :, :128], ends_recv[1, :, DEPTH:]], axis=0).astype(F32).T
            face_wide[1, LAST_SKIP : LAST_SKIP + FACE] = ahead[:FACE]
            face_mat[0] = face_wide[0, skip : skip + COEFS].astype(BF)
            face_mat[1] = face_wide[1, :COEFS].astype(BF)

        for copy in copies:
            copy.wait_recv()
        near = [near_recv.at[step, slot] for slot in (0, 1)]
        if step == 0:
            before, middle, after = whole_recv[0], weighted, whole_recv[1]
        else:
            before = sides[0] + near[0][own_part] + padded(far_recv[step - 1, 0], 1)
            middle = mine + padded(near[0][side_part], 1) + padded(near[1][side_part], 0)
            after = sides[1] + near[1][own_part] + padded(far_recv[step - 1, 1], 0)
            before, middle, after = before.astype(BF), middle.astype(BF), after.astype(BF)
        left = jnp.concatenate([before, middle], axis=0)
        right = jnp.concatenate([middle, after], axis=0)
        both = jnp.concatenate([left, right], axis=0)
        half = BLOCK // 2
        spread = jnp.concatenate([mm(spread_mat[:half], both), mm(spread_mat[half:], both)], axis=0)
        top = mm(face_mat[0], left)[:FACE_PAD] + near[0][face_part]
        bottom = mm(face_mat[1], right)[:FACE_PAD] + near[1][face_part]
        spread = jnp.concatenate(
            [
                spread[:FACE_PAD] + top,
                spread[FACE_PAD : BLOCK - FACE_PAD],
                spread[BLOCK - FACE_PAD :] + bottom,
            ],
            axis=0,
        )
        following = base_ref[...] + gain * spread
        if step < STEPS - 1:
            field[step + 1, :BLOCK, :] = following
            rounded = jnp.concatenate([following.astype(BF), jnp.zeros((FIELD - BLOCK, STATE_DEV), BF)], axis=0)
        else:
            out_x[...] = following[:NODE_DEV]

    high, low = split(following * following)
    loads[6].wait()
    weight = occ_ref[...] * (1.0 / (STATE_DEV * ns))
    weight_high = weight.astype(BF).astype(F32)
    row = lax.broadcasted_iota(jnp.int32, (16, STATE_DEV), 0)
    weights = jnp.where(row == 0, weight_high, jnp.where(row == 1, weight - weight_high, 0.0)).astype(BF)
    sums = mm_nt(weights, high) + mm_nt(weights, low)
    sums = sums[0:1] + sums[1:2]
    tiles = dens_send.shape[0]
    for tile in range(tiles):
        end = min(NODE_DEV, (tile + 1) * 128)
        dens_send[tile : tile + 1, : end - tile * 128] = sums[:, tile * 128 : end]
    if turns > 1:
        pl.semaphore_wait(token_sems.at[1], 2)
    dens_copies = []
    for shift in sorted(range(1, ns), key=lambda k: -min(k, ns - k)):
        dens_copies.append(send(dens_send, dens_recv.at[column], dens_sems, shift - 1, state_at(shift)))
    dens_recv[column] = dens_send[...]
    for copy in raw + ends + pending:
        copy.wait_send()
    for copy in dens_copies:
        copy.wait_recv()
    total = dens_recv[0]
    for peer in range(1, ns):
        total = total + dens_recv[peer]
    for tile in range(tiles):
        end = min(NODE_DEV, (tile + 1) * 128)
        out_d[tile * 128 : end] = total[tile, : end - tile * 128]
    for copy in dens_copies:
        copy.wait_send()


def store(x_ref, d_ref, x_hbm, d_hbm, sem):
    copies = [
        pltpu.make_async_copy(x_ref, x_hbm, sem.at[0]),
        pltpu.make_async_copy(d_ref, d_hbm, sem.at[1]),
    ]
    for copy in copies:
        copy.start()
    for copy in copies:
        copy.wait()


def solution(mesh):
    nc, ns = mesh.shape["cells"], mesh.shape["states"]

    def body(filter_input, cell_table, cell_type, atom_center, proj_values, coupling, occupation):
        any_space = pl.BlockSpec(memory_space=pl.ANY)
        vmem = pl.BlockSpec(memory_space=pltpu.VMEM)
        dma = pltpu.SemaphoreType.DMA
        filtered, density = pl.pallas_call(
            functools.partial(kernel, nc, ns),
            out_shape=(pltpu.VMEM((NODE_DEV, STATE_DEV), F32), pltpu.VMEM((NODE_DEV,), F32)),
            in_specs=[any_space] * 7,
            out_specs=(vmem, vmem),
            scratch_shapes=[
                pltpu.VMEM((NODE_DEV, STATE_DEV), BF),
                pltpu.VMEM((NODE_DEV - TAIL, STATE_DEV), BF),
                pltpu.VMEM((HEAD_ROWS, STATE_DEV), BF),
                pltpu.VMEM((CELL_NODES, NTYPE, CELL_NODES), BF),
                pltpu.SMEM(cell_type.shape, jnp.int32),
                pltpu.SMEM(atom_center.shape, jnp.int32),
                pltpu.VMEM(proj_values.shape, BF),
                pltpu.VMEM(coupling.shape, F32),
                pltpu.VMEM((1, STATE_DEV), F32),
                pltpu.VMEM((CELL_DEV, WIDE_ROWS, DEPTH), F32),
                pltpu.VMEM((CELL_DEV, ROWS, DEPTH), BF),
                pltpu.VMEM((CELL_DEV, COEFS, DEPTH), BF),
                pltpu.VMEM((CELL_DEV, 3 * COEFS + 2 * SIDE, DEPTH), BF),
                pltpu.VMEM((2, 2 * COEFS, DEPTH), BF),
                pltpu.VMEM((2, COEFS, DEPTH + 128), BF),
                pltpu.VMEM((2, COEFS, DEPTH + 128), BF),
                pltpu.VMEM((STRIDE + DEPTH + 2, 4 * COEFS), F32),
                pltpu.VMEM((BLOCK, 4 * COEFS), BF),
                pltpu.VMEM((2, 128, 2 * COEFS), F32),
                pltpu.VMEM((2, COEFS, 2 * COEFS), BF),
                pltpu.VMEM((STEPS, FIELD, STATE_DEV), F32),
                pltpu.VMEM((BLOCK, STATE_DEV), F32),
                pltpu.VMEM((STEPS, 2, NEAR_ROWS, STATE_DEV), F32),
                pltpu.VMEM((STEPS, 2, NEAR_ROWS, STATE_DEV), F32),
                pltpu.VMEM((STEPS - 1, 2, SIDE, STATE_DEV), F32),
                pltpu.VMEM((COEFS, STATE_DEV), BF),
                pltpu.VMEM((2, COEFS, STATE_DEV), BF),
                pltpu.VMEM((5, 128), F32),
                pltpu.VMEM((ns, 5, 128), F32),
                dma((7,)),
                dma((2, 2)),
                dma((2, 2)),
                dma((STEPS, 2, 2)),
                dma((2, 2)),
                dma((STEPS - 1, 2, 2)),
                dma((STEPS - 1, 2, 2)),
                dma((STEPS - 1, 2, 2)),
                dma((2, ns - 1)),
                pltpu.SemaphoreType.REGULAR((2,)),
            ],
            compiler_params=pltpu.CompilerParams(collective_id=0, has_side_effects=True),
        )(
            filter_input,
            jnp.swapaxes(cell_table, 0, 1),
            cell_type,
            atom_center,
            proj_values,
            coupling,
            occupation.reshape(1, STATE_DEV),
        )
        return pl.pallas_call(
            store,
            out_shape=(
                jax.ShapeDtypeStruct((NODE_DEV, STATE_DEV), F32),
                jax.ShapeDtypeStruct((NODE_DEV,), F32),
            ),
            in_specs=[any_space, any_space],
            out_specs=(any_space, any_space),
            scratch_shapes=[dma((2,))],
        )(*(pltpu.with_memory_space_constraint(v, pltpu.VMEM) for v in (filtered, density)))

    in_specs = (
        P("cells", "states"),
        P(),
        P("cells"),
        P("cells"),
        P("cells", None, None, None),
        P(),
        P("states"),
    )
    out_specs = (P("cells", "states"), P("cells"))
    return jax.shard_map(body, mesh=mesh, in_specs=in_specs, out_specs=out_specs, check_vma=False)
```

```python
import functools

import jax
import jax.numpy as jnp
from jax import lax
from jax.experimental import pallas as pl
from jax.experimental.pallas import tpu as pltpu
from jax.sharding import PartitionSpec as P

PROJECTORS = 16
STEPS = 3
FACE = 49
CELL_NODES = 343
STRIDE = 294
CELL_DEV = 2
NTYPE = 8
ATOM_DEV = 4
NODE_DEV = 637
STATE_DEV = 128
COEFS = ATOM_DEV * PROJECTORS

lower_edge = 4.0
upper_edge = 12.0
ground_edge = -2.0

DEPTH = 384
ROWS = 352
WIDE_ROWS = 368
BLOCK = 640
FIELD = 672
TAIL = 288
TAIL_SKIP = STRIDE - TAIL
HEAD_ROWS = 344
TAIL_COL = 256
FACE_PAD = 56
LAST_SKIP = NODE_DEV - FACE - (BLOCK - FACE_PAD)
SIDE = COEFS - PROJECTORS
NEAR_ROWS = COEFS + FACE_PAD + SIDE

BF = jnp.bfloat16
F32 = jnp.float32
MESH = pl.DeviceIdType.MESH


def mm(a, b):
    return jnp.dot(a, b, preferred_element_type=F32)


def mm_nt(a, b):
    return lax.dot_general(a, b, (((1,), (1,)), ((), ())), preferred_element_type=F32)


def scales():
    half_width = (upper_edge - lower_edge) / 2.0
    scale_now = half_width / (ground_edge - (upper_edge + lower_edge) / 2.0)
    twice_inverse = 2.0 / scale_now
    pairs = [(scale_now / half_width, 0.0)]
    for _ in range(STEPS - 1):
        scale_next = 1.0 / (twice_inverse - scale_now)
        pairs.append((2.0 * scale_next / half_width, scale_now * scale_next))
        scale_now = scale_next
    return pairs


def split(value):
    high = value.astype(BF)
    return high, (value - high.astype(F32)).astype(BF)


def kernel(
    nc,
    ns,
    x_hbm,
    tab_hbm,
    type_hbm,
    center_hbm,
    proj_hbm,
    coup_hbm,
    occ_hbm,
    out_x,
    out_d,
    xin,
    x_left,
    x_right,
    tab,
    types,
    centers,
    proj,
    coup_ref,
    occ_ref,
    hwide,
    hmat,
    own,
    probe,
    edge_mixed,
    ends_send,
    ends_recv,
    spread_wide,
    spread_mat,
    face_wide,
    face_mat,
    field,
    base_ref,
    near_send,
    near_recv,
    far_recv,
    whole_send,
    whole_recv,
    dens_send,
    dens_recv,
    load_sem,
    raw_sems,
    ends_sems,
    near_sems,
    whole_sems,
    far_sems,
    side_sems,
    dens_sems,
    token_sems,
):
    here = lax.axis_index("cells")
    column = lax.axis_index("states")

    def cell_at(shift):
        return {"cells": lax.rem(here + (shift + nc), nc)}

    def state_at(shift):
        return {"states": lax.rem(column + (shift + ns), ns)}

    barrier = pltpu.get_barrier_semaphore()
    for shift in (-1, 1):
        pl.semaphore_signal(barrier, inc=1, device_id=cell_at(shift), device_id_type=MESH)
        pl.semaphore_signal(barrier, inc=1, device_id=state_at(shift), device_id_type=MESH)

    sources = (center_hbm, proj_hbm, x_hbm, coup_hbm, type_hbm, tab_hbm, occ_hbm)
    targets = (centers, proj, xin, coup_ref, types, tab, occ_ref)
    loads = [pltpu.make_async_copy(*pair, load_sem.at[i]) for i, pair in enumerate(zip(sources, targets))]
    for load in loads:
        load.start()

    def send(src, dst, sems, slot, device):
        copy = pltpu.make_async_remote_copy(
            src_ref=src,
            dst_ref=dst,
            send_sem=sems.at[0, slot],
            recv_sem=sems.at[1, slot],
            device_id=device,
            device_id_type=MESH,
        )
        copy.start()
        return copy

    pl.semaphore_wait(barrier, 4)
    raw = [
        send(x_hbm.at[pl.ds(0, HEAD_ROWS)], x_right, raw_sems, 0, cell_at(-1)),
        send(x_hbm.at[pl.ds(TAIL, NODE_DEV - TAIL)], x_left, raw_sems, 1, cell_at(1)),
    ]

    def tell(turn):
        for shift in (-1 - turn, 1 + turn):
            pl.semaphore_signal(token_sems.at[turn], inc=1, device_id=state_at(shift), device_id_type=MESH)

    turns = 2 if ns > 5 else (1 if ns > 3 else 0)
    if turns > 0:
        tell(0)

    own[...] = jnp.zeros_like(own)
    ends_send[...] = jnp.zeros_like(ends_send)

    loads[0].wait()
    loads[1].wait()
    spots = [centers[atom] for atom in range(ATOM_DEV)]
    on_last = sum(spots)
    on_first = ATOM_DEV - on_last
    places = []
    for atom in range(ATOM_DEV):
        ones = sum(spots[:atom]) if atom else 0
        places.append(jnp.where(spots[atom] == 0, atom - ones, on_first + ones))
    for rank in range(ATOM_DEV):
        atom = sum(jnp.where(places[k] == rank, k, 0) for k in range(ATOM_DEV))
        first = rank < on_first
        rows = pl.ds(rank * PROJECTORS, PROJECTORS)
        before, middle, after = (proj[atom, j].astype(F32) for j in range(3))
        zero = jnp.zeros_like(before)
        own[0, rows, :CELL_NODES] = jnp.where(first, middle, before).astype(BF)
        own[1, rows, :CELL_NODES] = jnp.where(first, after, middle).astype(BF)
        if rank < ATOM_DEV - 1:
            ends_send[0, rows, :CELL_NODES] = jnp.where(first, before, zero).astype(BF)
        if rank > 0:
            ends_send[1, rows, :CELL_NODES] = jnp.where(first, zero, after).astype(BF)
    ends_send[0, :, DEPTH:] = own[0, :, :128]
    ends_send[1, :, DEPTH:] = own[1, :, TAIL_COL:]
    ends = [
        send(ends_send.at[0], ends_recv.at[1], ends_sems, 0, cell_at(-1)),
        send(ends_send.at[1], ends_recv.at[0], ends_sems, 1, cell_at(1)),
    ]

    field[:, NODE_DEV - 5 :, :] = jnp.zeros((STEPS, FIELD - NODE_DEV + 5, STATE_DEV), F32)
    hwide[...] = jnp.zeros_like(hwide)
    spread_wide[...] = jnp.zeros_like(spread_wide)
    face_wide[...] = jnp.zeros_like(face_wide)
    dens_send[...] = jnp.zeros_like(dens_send)
    loads[2].wait()
    field[0, :NODE_DEV, :] = xin[...].astype(F32)

    loads[3].wait()
    pick = (
        lax.rem(lax.broadcasted_iota(jnp.int32, (COEFS, PROJECTORS), 0), PROJECTORS)
        == lax.broadcasted_iota(jnp.int32, (COEFS, PROJECTORS), 1)
    )
    pick = jnp.where(pick, 1.0, 0.0).astype(BF)
    same = lax.div(lax.broadcasted_iota(jnp.int32, (COEFS, COEFS), 0), PROJECTORS) == lax.div(
        lax.broadcasted_iota(jnp.int32, (COEFS, COEFS), 1), PROJECTORS
    )
    mix_high, mix_low = (
        jnp.where(same, mm_nt(mm(pick, piece).astype(BF), pick), 0.0).astype(BF) for piece in split(coup_ref[...])
    )

    def mixed(rows):
        return mm(mix_high, rows) + mm(mix_low, rows)

    def fold(both):
        half = both.shape[0] // 2
        return both[:half] + both[half:]

    def moved(value, cell):
        return pltpu.roll(value, TAIL_SKIP, 1) if cell else value

    for cell in range(CELL_DEV):
        probe[cell, :COEFS], probe[cell, COEFS : 2 * COEFS] = split(moved(mixed(own[cell]), cell))
        edge_mixed[cell, :COEFS], edge_mixed[cell, COEFS:] = split(
            moved(mixed(ends_send[cell, :, :DEPTH]), 1 - cell)
        )

    faces = slice(2 * COEFS, 3 * COEFS)
    loads[4].wait()
    loads[5].wait()
    chunk = 256 // NTYPE
    spot = lax.broadcasted_iota(jnp.int32, (CELL_DEV * chunk, 256), 0)
    kind = jnp.where(spot < chunk, types[0], types[1])
    take = lax.broadcasted_iota(jnp.int32, (CELL_DEV * chunk, 256), 1) == lax.rem(spot, chunk) * NTYPE + kind
    take = jnp.where(take, 1.0, 0.0).astype(BF)
    for start in range(0, CELL_NODES, chunk):
        count = min(chunk, CELL_NODES - start)
        entries = tab[start : start + count].reshape(count * NTYPE, CELL_NODES)
        rows = mm(take[:, : count * NTYPE], entries)
        for cell in range(CELL_DEV):
            begin = start + cell * TAIL_SKIP
            hwide[cell, begin : begin + count, :CELL_NODES] = rows[cell * chunk : cell * chunk + count]
    hwide[1] = moved(hwide[1], 1)
    hmat[...] = hwide[:, :ROWS].astype(BF)
    probe[1, faces] = hwide[1, STRIDE + TAIL_SKIP : STRIDE + TAIL_SKIP + COEFS].astype(BF)
    hwide[0, LAST_SKIP : LAST_SKIP + FACE] = hwide[0, :FACE]
    hwide[0, :LAST_SKIP] = jnp.zeros((LAST_SKIP, DEPTH), F32)
    hwide[0, LAST_SKIP + FACE : COEFS] = jnp.zeros((COEFS - LAST_SKIP - FACE, DEPTH), F32)
    probe[0, faces] = hwide[0, :COEFS].astype(BF)

    own_part = slice(0, COEFS)
    face_part = slice(COEFS, COEFS + FACE_PAD)
    side_part = slice(COEFS + FACE_PAD, NEAR_ROWS)
    blank = jnp.zeros((PROJECTORS, STATE_DEV), F32)

    def padded(side, slot):
        return jnp.concatenate([side, blank] if slot else [blank, side], axis=0)

    pending = []
    rounded = field[0].astype(BF)
    for step, (gain, back) in enumerate(scales()):
        x = field.at[step]
        cells = (rounded[:DEPTH], rounded[TAIL:])
        copies = []

        def exchange(part, sems):
            rows = pl.ds(part.start, part.stop - part.start)
            for slot, shift in ((1, 1), (0, -1)):
                copies.append(
                    send(
                        near_send.at[step, slot, rows],
                        near_recv.at[step, 1 - slot, rows],
                        sems,
                        slot,
                        cell_at(shift),
                    )
                )

        sides = [None, None]
        if step:
            for slot, shift in ((1, 1), (0, -1)):
                side = fold(mm(probe[slot, 3 * COEFS :], cells[slot]))
                near_send[step, slot, side_part] = side
                sides[slot] = padded(side, slot)
                copies.append(
                    send(
                        near_send.at[step, slot, pl.ds(side_part.start, SIDE)],
                        far_recv.at[step - 1, 1 - slot],
                        far_sems.at[step - 1],
                        slot,
                        cell_at(2 * shift),
                    )
                )
            exchange(side_part, side_sems.at[step - 1])
        mine = fold(mm(probe[0, : 2 * COEFS], cells[0]) + mm(probe[1, : 2 * COEFS], cells[1]))
        if step:
            for slot in (0, 1):
                near_send[step, slot, own_part] = mine
        for slot in (0, 1):
            near_send[step, slot, face_part] = mm(probe[slot, faces], cells[slot])[:FACE_PAD]
        exchange(slice(0, face_part.stop) if step else face_part, near_sems.at[step])

        if step == 0:
            for copy in raw:
                copy.wait_recv()
            edges = mm(edge_mixed[0, :, : NODE_DEV - TAIL], x_left[...])
            edges = edges + mm(edge_mixed[1, :, :HEAD_ROWS], x_right[...])
            weighted = (mine + fold(edges)).astype(BF)
            whole_send[...] = weighted
            copies += [
                send(whole_send, whole_recv.at[1 - slot], whole_sems, slot, cell_at(shift))
                for slot, shift in ((0, -1), (1, 1))
            ]
        pending += copies
        if step == 1 and turns > 0:
            pl.semaphore_wait(token_sems.at[0], 2)
            if turns > 1:
                tell(1)

        centre = (upper_edge + lower_edge) / 2.0
        base = (-centre * gain) * x[:BLOCK, :]
        if step:
            base = base - back * field[step - 1, :BLOCK, :]
        base_ref[...] = base
        base_ref[:ROWS, :] += gain * mm(hmat[0], cells[0])
        base_ref[TAIL:, :] += gain * mm(hmat[1], cells[1])

        if step == 0:
            for copy in ends:
                copy.wait_recv()
            for slot in (0, 1):
                skip = PROJECTORS * (1 - slot)
                side = moved(mixed(ends_recv[slot, :, :DEPTH])[skip : skip + SIDE], slot)
                probe[slot, 3 * COEFS : 3 * COEFS + SIDE], probe[slot, 3 * COEFS + SIDE :] = split(side)
            spread_wide[:DEPTH, : 2 * COEFS] = (
                jnp.concatenate([ends_recv[0, :, :DEPTH], own[0]], axis=0).astype(F32).T
            )
            spread_wide[STRIDE : STRIDE + DEPTH, 2 * COEFS :] = (
                jnp.concatenate([own[1], ends_recv[1, :, :DEPTH]], axis=0).astype(F32).T
            )
            spread_mat[...] = spread_wide[:BLOCK].astype(BF)
            skip = STRIDE - TAIL_COL
            face_wide[0, :128] = (
                jnp.concatenate([ends_recv[0, :, DEPTH:], ends_send[0, :, TAIL_COL:DEPTH]], axis=0).astype(F32).T
            )
            ahead = jnp.concatenate([ends_send[1, :, :128], ends_recv[1, :, DEPTH:]], axis=0).astype(F32).T
            face_wide[1, LAST_SKIP : LAST_SKIP + FACE] = ahead[:FACE]
            face_mat[0] = face_wide[0, skip : skip + COEFS].astype(BF)
            face_mat[1] = face_wide[1, :COEFS].astype(BF)

        for copy in copies:
            copy.wait_recv()
        near = [near_recv.at[step, slot] for slot in (0, 1)]
        if step == 0:
            before, middle, after = whole_recv[0], weighted, whole_recv[1]
        else:
            before = sides[0] + near[0][own_part] + padded(far_recv[step - 1, 0], 1)
            middle = mine + padded(near[0][side_part], 1) + padded(near[1][side_part], 0)
            after = sides[1] + near[1][own_part] + padded(far_recv[step - 1, 1], 0)
            before, middle, after = before.astype(BF), middle.astype(BF), after.astype(BF)
        left = jnp.concatenate([before, middle], axis=0)
        right = jnp.concatenate([middle, after], axis=0)
        both = jnp.concatenate([left, right], axis=0)
        half = BLOCK // 2
        spread = jnp.concatenate([mm(spread_mat[:half], both), mm(spread_mat[half:], both)], axis=0)
        top = mm(face_mat[0], left)[:FACE_PAD] + near[0][face_part]
        bottom = mm(face_mat[1], right)[:FACE_PAD] + near[1][face_part]
        spread = jnp.concatenate(
            [
                spread[:FACE_PAD] + top,
                spread[FACE_PAD : BLOCK - FACE_PAD],
                spread[BLOCK - FACE_PAD :] + bottom,
            ],
            axis=0,
        )
        following = base_ref[...] + gain * spread
        if step < STEPS - 1:
            field[step + 1, :BLOCK, :] = following
            rounded = jnp.concatenate([following.astype(BF), jnp.zeros((FIELD - BLOCK, STATE_DEV), BF)], axis=0)
        else:
            out_x[...] = following[:NODE_DEV]

    high, low = split(following * following)
    loads[6].wait()
    weight = occ_ref[...] * (1.0 / (STATE_DEV * ns))
    weight_high = weight.astype(BF).astype(F32)
    row = lax.broadcasted_iota(jnp.int32, (16, STATE_DEV), 0)
    weights = jnp.where(row == 0, weight_high, jnp.where(row == 1, weight - weight_high, 0.0)).astype(BF)
    sums = mm_nt(weights, high) + mm_nt(weights, low)
    sums = sums[0:1] + sums[1:2]
    tiles = dens_send.shape[0]
    for tile in range(tiles):
        end = min(NODE_DEV, (tile + 1) * 128)
        dens_send[tile : tile + 1, : end - tile * 128] = sums[:, tile * 128 : end]
    if turns > 1:
        pl.semaphore_wait(token_sems.at[1], 2)
    dens_copies = []
    for shift in sorted(range(1, ns), key=lambda k: -min(k, ns - k)):
        dens_copies.append(send(dens_send, dens_recv.at[column], dens_sems, shift - 1, state_at(shift)))
    dens_recv[column] = dens_send[...]
    for copy in raw + ends + pending:
        copy.wait_send()
    for copy in dens_copies:
        copy.wait_recv()
    total = dens_recv[0]
    for peer in range(1, ns):
        total = total + dens_recv[peer]
    for tile in range(tiles):
        end = min(NODE_DEV, (tile + 1) * 128)
        out_d[tile * 128 : end] = total[tile, : end - tile * 128]
    for copy in dens_copies:
        copy.wait_send()


def store(x_ref, d_ref, x_hbm, d_hbm, sem):
    copies = [
        pltpu.make_async_copy(x_ref, x_hbm, sem.at[0]),
        pltpu.make_async_copy(d_ref, d_hbm, sem.at[1]),
    ]
    for copy in copies:
        copy.start()
    for copy in copies:
        copy.wait()


def solution(mesh):
    nc, ns = mesh.shape["cells"], mesh.shape["states"]

    def body(filter_input, cell_table, cell_type, atom_center, proj_values, coupling, occupation):
        any_space = pl.BlockSpec(memory_space=pl.ANY)
        vmem = pl.BlockSpec(memory_space=pltpu.VMEM)
        dma = pltpu.SemaphoreType.DMA
        filtered, density = pl.pallas_call(
            functools.partial(kernel, nc, ns),
            out_shape=(pltpu.VMEM((NODE_DEV, STATE_DEV), F32), pltpu.VMEM((NODE_DEV,), F32)),
            in_specs=[any_space] * 7,
            out_specs=(vmem, vmem),
            scratch_shapes=[
                pltpu.VMEM((NODE_DEV, STATE_DEV), BF),
                pltpu.VMEM((NODE_DEV - TAIL, STATE_DEV), BF),
                pltpu.VMEM((HEAD_ROWS, STATE_DEV), BF),
                pltpu.VMEM((CELL_NODES, NTYPE, CELL_NODES), BF),
                pltpu.SMEM(cell_type.shape, jnp.int32),
                pltpu.SMEM(atom_center.shape, jnp.int32),
                pltpu.VMEM(proj_values.shape, BF),
                pltpu.VMEM(coupling.shape, F32),
                pltpu.VMEM((1, STATE_DEV), F32),
                pltpu.VMEM((CELL_DEV, WIDE_ROWS, DEPTH), F32),
                pltpu.VMEM((CELL_DEV, ROWS, DEPTH), BF),
                pltpu.VMEM((CELL_DEV, COEFS, DEPTH), BF),
                pltpu.VMEM((CELL_DEV, 3 * COEFS + 2 * SIDE, DEPTH), BF),
                pltpu.VMEM((2, 2 * COEFS, DEPTH), BF),
                pltpu.VMEM((2, COEFS, DEPTH + 128), BF),
                pltpu.VMEM((2, COEFS, DEPTH + 128), BF),
                pltpu.VMEM((STRIDE + DEPTH + 2, 4 * COEFS), F32),
                pltpu.VMEM((BLOCK, 4 * COEFS), BF),
                pltpu.VMEM((2, 128, 2 * COEFS), F32),
                pltpu.VMEM((2, COEFS, 2 * COEFS), BF),
                pltpu.VMEM((STEPS, FIELD, STATE_DEV), F32),
                pltpu.VMEM((BLOCK, STATE_DEV), F32),
                pltpu.VMEM((STEPS, 2, NEAR_ROWS, STATE_DEV), F32),
                pltpu.VMEM((STEPS, 2, NEAR_ROWS, STATE_DEV), F32),
                pltpu.VMEM((STEPS - 1, 2, SIDE, STATE_DEV), F32),
                pltpu.VMEM((COEFS, STATE_DEV), BF),
                pltpu.VMEM((2, COEFS, STATE_DEV), BF),
                pltpu.VMEM((5, 128), F32),
                pltpu.VMEM((ns, 5, 128), F32),
                dma((7,)),
                dma((2, 2)),
                dma((2, 2)),
                dma((STEPS, 2, 2)),
                dma((2, 2)),
                dma((STEPS - 1, 2, 2)),
                dma((STEPS - 1, 2, 2)),
                dma((2, ns - 1)),
                pltpu.SemaphoreType.REGULAR((2,)),
            ],
            compiler_params=pltpu.CompilerParams(collective_id=0, has_side_effects=True),
        )(
            filter_input,
            jnp.swapaxes(cell_table, 0, 1),
            cell_type,
            atom_center,
            proj_values,
            coupling,
            occupation.reshape(1, STATE_DEV),
        )
        return pl.pallas_call(
            store,
            out_shape=(
                jax.ShapeDtypeStruct((NODE_DEV, STATE_DEV), F32),
                jax.ShapeDtypeStruct((NODE_DEV,), F32),
            ),
            in_specs=[any_space, any_space],
            out_specs=(any_space, any_space),
            scratch_shapes=[dma((2,))],
        )(*(pltpu.with_memory_space_constraint(v, pltpu.VMEM) for v in (filtered, density)))

    in_specs = (
        P("cells", "states"),
        P(),
        P("cells"),
        P("cells"),
        P("cells", None, None, None),
        P(),
        P("states"),
    )
    out_specs = (P("cells", "states"), P("cells"))
    return jax.shard_map(body, mesh=mesh, in_specs=in_specs, out_specs=out_specs, check_vma=False)
```

```python
import functools

import jax
import jax.numpy as jnp
from jax import lax
from jax.experimental import pallas as pl
from jax.experimental.pallas import tpu as pltpu
from jax.sharding import PartitionSpec as P

PROJECTORS = 16
STEPS = 3
FACE = 49
CELL_NODES = 343
STRIDE = 294
CELL_DEV = 2
NTYPE = 8
ATOM_DEV = 4
NODE_DEV = 637
STATE_DEV = 128
COEFS = ATOM_DEV * PROJECTORS

lower_edge = 4.0
upper_edge = 12.0
ground_edge = -2.0

DEPTH = 384
ROWS = 352
WIDE_ROWS = 368
BLOCK = 640
FIELD = 672
TAIL = 288
TAIL_SKIP = STRIDE - TAIL
HEAD_ROWS = 344
TAIL_COL = 256
FACE_PAD = 56
LAST_SKIP = NODE_DEV - FACE - (BLOCK - FACE_PAD)
SIDE = COEFS - PROJECTORS
NEAR_ROWS = COEFS + FACE_PAD + SIDE

BF = jnp.bfloat16
F32 = jnp.float32
MESH = pl.DeviceIdType.MESH


def mm(a, b):
    return jnp.dot(a, b, preferred_element_type=F32)


def mm_nt(a, b):
    return lax.dot_general(a, b, (((1,), (1,)), ((), ())), preferred_element_type=F32)


def scales():
    half_width = (upper_edge - lower_edge) / 2.0
    scale_now = half_width / (ground_edge - (upper_edge + lower_edge) / 2.0)
    twice_inverse = 2.0 / scale_now
    pairs = [(scale_now / half_width, 0.0)]
    for _ in range(STEPS - 1):
        scale_next = 1.0 / (twice_inverse - scale_now)
        pairs.append((2.0 * scale_next / half_width, scale_now * scale_next))
        scale_now = scale_next
    return pairs


def split(value):
    high = value.astype(BF)
    return high, (value - high.astype(F32)).astype(BF)


def kernel(
    nc,
    ns,
    x_hbm,
    tab_hbm,
    type_hbm,
    center_hbm,
    proj_hbm,
    coup_hbm,
    occ_hbm,
    out_x,
    out_d,
    xin,
    x_left,
    x_right,
    tab,
    types,
    centers,
    proj,
    coup_ref,
    occ_ref,
    hwide,
    hmat,
    own,
    probe,
    edge_mixed,
    ends_send,
    ends_recv,
    spread_wide,
    spread_mat,
    face_wide,
    face_mat,
    field,
    base_ref,
    near_send,
    near_recv,
    far_recv,
    whole_send,
    whole_recv,
    dens_send,
    dens_recv,
    load_sem,
    raw_sems,
    ends_sems,
    near_sems,
    whole_sems,
    far_sems,
    side_sems,
    dens_sems,
    token_sems,
):
    here = lax.axis_index("cells")
    column = lax.axis_index("states")

    def cell_at(shift):
        return {"cells": lax.rem(here + (shift + nc), nc)}

    def state_at(shift):
        return {"states": lax.rem(column + (shift + ns), ns)}

    barrier = pltpu.get_barrier_semaphore()
    for shift in (-1, 1):
        pl.semaphore_signal(barrier, inc=1, device_id=cell_at(shift), device_id_type=MESH)
        pl.semaphore_signal(barrier, inc=1, device_id=state_at(shift), device_id_type=MESH)

    sources = (center_hbm, proj_hbm, x_hbm, coup_hbm, type_hbm, tab_hbm, occ_hbm)
    targets = (centers, proj, xin, coup_ref, types, tab, occ_ref)
    loads = [pltpu.make_async_copy(*pair, load_sem.at[i]) for i, pair in enumerate(zip(sources, targets))]
    for load in loads:
        load.start()

    def send(src, dst, sems, slot, device):
        copy = pltpu.make_async_remote_copy(
            src_ref=src,
            dst_ref=dst,
            send_sem=sems.at[0, slot],
            recv_sem=sems.at[1, slot],
            device_id=device,
            device_id_type=MESH,
        )
        copy.start()
        return copy

    pl.semaphore_wait(barrier, 4)
    raw = [
        send(x_hbm.at[pl.ds(TAIL, NODE_DEV - TAIL)], x_left, raw_sems, 1, cell_at(1)),
        send(x_hbm.at[pl.ds(0, HEAD_ROWS)], x_right, raw_sems, 0, cell_at(-1)),
    ]

    def tell(turn):
        for shift in (-1 - turn, 1 + turn):
            pl.semaphore_signal(token_sems.at[turn], inc=1, device_id=state_at(shift), device_id_type=MESH)

    turns = 2 if ns > 5 else (1 if ns > 3 else 0)
    if turns > 0:
        tell(0)

    own[...] = jnp.zeros_like(own)
    ends_send[...] = jnp.zeros_like(ends_send)

    loads[0].wait()
    loads[1].wait()
    spots = [centers[atom] for atom in range(ATOM_DEV)]
    on_last = sum(spots)
    on_first = ATOM_DEV - on_last
    places = []
    for atom in range(ATOM_DEV):
        ones = sum(spots[:atom]) if atom else 0
        places.append(jnp.where(spots[atom] == 0, atom - ones, on_first + ones))
    for rank in range(ATOM_DEV):
        atom = sum(jnp.where(places[k] == rank, k, 0) for k in range(ATOM_DEV))
        first = rank < on_first
        rows = pl.ds(rank * PROJECTORS, PROJECTORS)
        before, middle, after = (proj[atom, j].astype(F32) for j in range(3))
        zero = jnp.zeros_like(before)
        own[0, rows, :CELL_NODES] = jnp.where(first, middle, before).astype(BF)
        own[1, rows, :CELL_NODES] = jnp.where(first, after, middle).astype(BF)
        if rank < ATOM_DEV - 1:
            ends_send[0, rows, :CELL_NODES] = jnp.where(first, before, zero).astype(BF)
        if rank > 0:
            ends_send[1, rows, :CELL_NODES] = jnp.where(first, zero, after).astype(BF)
    ends_send[0, :, DEPTH:] = own[0, :, :128]
    ends_send[1, :, DEPTH:] = own[1, :, TAIL_COL:]
    ends = [
        send(ends_send.at[1], ends_recv.at[0], ends_sems, 1, cell_at(1)),
        send(ends_send.at[0], ends_recv.at[1], ends_sems, 0, cell_at(-1)),
    ]

    field[:, NODE_DEV - 5 :, :] = jnp.zeros((STEPS, FIELD - NODE_DEV + 5, STATE_DEV), F32)
    hwide[...] = jnp.zeros_like(hwide)
    spread_wide[...] = jnp.zeros_like(spread_wide)
    face_wide[...] = jnp.zeros_like(face_wide)
    dens_send[...] = jnp.zeros_like(dens_send)
    loads[2].wait()
    field[0, :NODE_DEV, :] = xin[...].astype(F32)

    loads[3].wait()
    pick = (
        lax.rem(lax.broadcasted_iota(jnp.int32, (COEFS, PROJECTORS), 0), PROJECTORS)
        == lax.broadcasted_iota(jnp.int32, (COEFS, PROJECTORS), 1)
    )
    pick = jnp.where(pick, 1.0, 0.0).astype(BF)
    same = lax.div(lax.broadcasted_iota(jnp.int32, (COEFS, COEFS), 0), PROJECTORS) == lax.div(
        lax.broadcasted_iota(jnp.int32, (COEFS, COEFS), 1), PROJECTORS
    )
    mix_high, mix_low = (
        jnp.where(same, mm_nt(mm(pick, piece).astype(BF), pick), 0.0).astype(BF) for piece in split(coup_ref[...])
    )

    def mixed(rows):
        return mm(mix_high, rows) + mm(mix_low, rows)

    def fold(both):
        half = both.shape[0] // 2
        return both[:half] + both[half:]

    def moved(value, cell):
        return pltpu.roll(value, TAIL_SKIP, 1) if cell else value

    for cell in range(CELL_DEV):
        probe[cell, :COEFS], probe[cell, COEFS : 2 * COEFS] = split(moved(mixed(own[cell]), cell))
        edge_mixed[cell, :COEFS], edge_mixed[cell, COEFS:] = split(
            moved(mixed(ends_send[cell, :, :DEPTH]), 1 - cell)
        )

    faces = slice(2 * COEFS, 3 * COEFS)
    loads[4].wait()
    loads[5].wait()
    chunk = 256 // NTYPE
    spot = lax.broadcasted_iota(jnp.int32, (CELL_DEV * chunk, 256), 0)
    kind = jnp.where(spot < chunk, types[0], types[1])
    take = lax.broadcasted_iota(jnp.int32, (CELL_DEV * chunk, 256), 1) == lax.rem(spot, chunk) * NTYPE + kind
    take = jnp.where(take, 1.0, 0.0).astype(BF)
    for start in range(0, CELL_NODES, chunk):
        count = min(chunk, CELL_NODES - start)
        entries = tab[start : start + count].reshape(count * NTYPE, CELL_NODES)
        rows = mm(take[:, : count * NTYPE], entries)
        for cell in range(CELL_DEV):
            begin = start + cell * TAIL_SKIP
            hwide[cell, begin : begin + count, :CELL_NODES] = rows[cell * chunk : cell * chunk + count]
    hwide[1] = moved(hwide[1], 1)
    hmat[...] = hwide[:, :ROWS].astype(BF)
    probe[1, faces] = hwide[1, STRIDE + TAIL_SKIP : STRIDE + TAIL_SKIP + COEFS].astype(BF)
    hwide[0, LAST_SKIP : LAST_SKIP + FACE] = hwide[0, :FACE]
    hwide[0, :LAST_SKIP] = jnp.zeros((LAST_SKIP, DEPTH), F32)
    hwide[0, LAST_SKIP + FACE : COEFS] = jnp.zeros((COEFS - LAST_SKIP - FACE, DEPTH), F32)
    probe[0, faces] = hwide[0, :COEFS].astype(BF)

    own_part = slice(0, COEFS)
    face_part = slice(COEFS, COEFS + FACE_PAD)
    side_part = slice(COEFS + FACE_PAD, NEAR_ROWS)
    blank = jnp.zeros((PROJECTORS, STATE_DEV), F32)

    def padded(side, slot):
        return jnp.concatenate([side, blank] if slot else [blank, side], axis=0)

    pending = []
    rounded = field[0].astype(BF)
    for step, (gain, back) in enumerate(scales()):
        x = field.at[step]
        cells = (rounded[:DEPTH], rounded[TAIL:])
        copies = []

        def exchange(part, sems):
            rows = pl.ds(part.start, part.stop - part.start)
            for slot, shift in ((1, 1), (0, -1)):
                copies.append(
                    send(
                        near_send.at[step, slot, rows],
                        near_recv.at[step, 1 - slot, rows],
                        sems,
                        slot,
                        cell_at(shift),
                    )
                )

        sides = [None, None]
        if step:
            for slot, shift in ((1, 1), (0, -1)):
                side = fold(mm(probe[slot, 3 * COEFS :], cells[slot]))
                near_send[step, slot, side_part] = side
                sides[slot] = padded(side, slot)
                copies.append(
                    send(
                        near_send.at[step, slot, pl.ds(side_part.start, SIDE)],
                        far_recv.at[step - 1, 1 - slot],
                        far_sems.at[step - 1],
                        slot,
                        cell_at(2 * shift),
                    )
                )
            exchange(side_part, side_sems.at[step - 1])
        mine = fold(mm(probe[0, : 2 * COEFS], cells[0]) + mm(probe[1, : 2 * COEFS], cells[1]))
        if step:
            for slot in (0, 1):
                near_send[step, slot, own_part] = mine
        for slot in (0, 1):
            near_send[step, slot, face_part] = mm(probe[slot, faces], cells[slot])[:FACE_PAD]
        exchange(slice(0, face_part.stop) if step else face_part, near_sems.at[step])

        if step == 0:
            for copy in raw:
                copy.wait_recv()
            edges = mm(edge_mixed[0, :, : NODE_DEV - TAIL], x_left[...])
            edges = edges + mm(edge_mixed[1, :, :HEAD_ROWS], x_right[...])
            weighted = (mine + fold(edges)).astype(BF)
            whole_send[...] = weighted
            copies += [
                send(whole_send, whole_recv.at[1 - slot], whole_sems, slot, cell_at(shift))
                for slot, shift in ((1, 1), (0, -1))
            ]
        pending += copies
        if step == 1 and turns > 0:
            pl.semaphore_wait(token_sems.at[0], 2)
            if turns > 1:
                tell(1)

        centre = (upper_edge + lower_edge) / 2.0
        base = (-centre * gain) * x[:BLOCK, :]
        if step:
            base = base - back * field[step - 1, :BLOCK, :]
        base_ref[...] = base
        base_ref[:ROWS, :] += gain * mm(hmat[0], cells[0])
        base_ref[TAIL:, :] += gain * mm(hmat[1], cells[1])

        if step == 0:
            for copy in ends:
                copy.wait_recv()
            for slot in (0, 1):
                skip = PROJECTORS * (1 - slot)
                side = moved(mixed(ends_recv[slot, :, :DEPTH])[skip : skip + SIDE], slot)
                probe[slot, 3 * COEFS : 3 * COEFS + SIDE], probe[slot, 3 * COEFS + SIDE :] = split(side)
            spread_wide[:DEPTH, : 2 * COEFS] = (
                jnp.concatenate([ends_recv[0, :, :DEPTH], own[0]], axis=0).astype(F32).T
            )
            spread_wide[STRIDE : STRIDE + DEPTH, 2 * COEFS :] = (
                jnp.concatenate([own[1], ends_recv[1, :, :DEPTH]], axis=0).astype(F32).T
            )
            spread_mat[...] = spread_wide[:BLOCK].astype(BF)
            skip = STRIDE - TAIL_COL
            face_wide[0, :128] = (
                jnp.concatenate([ends_recv[0, :, DEPTH:], ends_send[0, :, TAIL_COL:DEPTH]], axis=0).astype(F32).T
            )
            ahead = jnp.concatenate([ends_send[1, :, :128], ends_recv[1, :, DEPTH:]], axis=0).astype(F32).T
            face_wide[1, LAST_SKIP : LAST_SKIP + FACE] = ahead[:FACE]
            face_mat[0] = face_wide[0, skip : skip + COEFS].astype(BF)
            face_mat[1] = face_wide[1, :COEFS].astype(BF)

        for copy in copies:
            copy.wait_recv()
        near = [near_recv.at[step, slot] for slot in (0, 1)]
        if step == 0:
            before, middle, after = whole_recv[0], weighted, whole_recv[1]
        else:
            before = sides[0] + near[0][own_part] + padded(far_recv[step - 1, 0], 1)
            middle = mine + padded(near[0][side_part], 1) + padded(near[1][side_part], 0)
            after = sides[1] + near[1][own_part] + padded(far_recv[step - 1, 1], 0)
            before, middle, after = before.astype(BF), middle.astype(BF), after.astype(BF)
        left = jnp.concatenate([before, middle], axis=0)
        right = jnp.concatenate([middle, after], axis=0)
        both = jnp.concatenate([left, right], axis=0)
        half = BLOCK // 2
        spread = jnp.concatenate([mm(spread_mat[:half], both), mm(spread_mat[half:], both)], axis=0)
        top = mm(face_mat[0], left)[:FACE_PAD] + near[0][face_part]
        bottom = mm(face_mat[1], right)[:FACE_PAD] + near[1][face_part]
        spread = jnp.concatenate(
            [
                spread[:FACE_PAD] + top,
                spread[FACE_PAD : BLOCK - FACE_PAD],
                spread[BLOCK - FACE_PAD :] + bottom,
            ],
            axis=0,
        )
        following = base_ref[...] + gain * spread
        if step < STEPS - 1:
            field[step + 1, :BLOCK, :] = following
            rounded = jnp.concatenate([following.astype(BF), jnp.zeros((FIELD - BLOCK, STATE_DEV), BF)], axis=0)
        else:
            out_x[...] = following[:NODE_DEV]

    high, low = split(following * following)
    loads[6].wait()
    weight = occ_ref[...] * (1.0 / (STATE_DEV * ns))
    weight_high = weight.astype(BF).astype(F32)
    row = lax.broadcasted_iota(jnp.int32, (16, STATE_DEV), 0)
    weights = jnp.where(row == 0, weight_high, jnp.where(row == 1, weight - weight_high, 0.0)).astype(BF)
    sums = mm_nt(weights, high) + mm_nt(weights, low)
    sums = sums[0:1] + sums[1:2]
    tiles = dens_send.shape[0]
    for tile in range(tiles):
        end = min(NODE_DEV, (tile + 1) * 128)
        dens_send[tile : tile + 1, : end - tile * 128] = sums[:, tile * 128 : end]
    if turns > 1:
        pl.semaphore_wait(token_sems.at[1], 2)
    dens_copies = []
    for shift in sorted(range(1, ns), key=lambda k: -min(k, ns - k)):
        dens_copies.append(send(dens_send, dens_recv.at[column], dens_sems, shift - 1, state_at(shift)))
    dens_recv[column] = dens_send[...]
    for copy in raw + ends + pending:
        copy.wait_send()
    for copy in dens_copies:
        copy.wait_recv()
    total = dens_recv[0]
    for peer in range(1, ns):
        total = total + dens_recv[peer]
    for tile in range(tiles):
        end = min(NODE_DEV, (tile + 1) * 128)
        out_d[tile * 128 : end] = total[tile, : end - tile * 128]
    for copy in dens_copies:
        copy.wait_send()


def store(x_ref, d_ref, x_hbm, d_hbm, sem):
    copies = [
        pltpu.make_async_copy(x_ref, x_hbm, sem.at[0]),
        pltpu.make_async_copy(d_ref, d_hbm, sem.at[1]),
    ]
    for copy in copies:
        copy.start()
    for copy in copies:
        copy.wait()


def solution(mesh):
    nc, ns = mesh.shape["cells"], mesh.shape["states"]

    def body(filter_input, cell_table, cell_type, atom_center, proj_values, coupling, occupation):
        any_space = pl.BlockSpec(memory_space=pl.ANY)
        vmem = pl.BlockSpec(memory_space=pltpu.VMEM)
        dma = pltpu.SemaphoreType.DMA
        filtered, density = pl.pallas_call(
            functools.partial(kernel, nc, ns),
            out_shape=(pltpu.VMEM((NODE_DEV, STATE_DEV), F32), pltpu.VMEM((NODE_DEV,), F32)),
            in_specs=[any_space] * 7,
            out_specs=(vmem, vmem),
            scratch_shapes=[
                pltpu.VMEM((NODE_DEV, STATE_DEV), BF),
                pltpu.VMEM((NODE_DEV - TAIL, STATE_DEV), BF),
                pltpu.VMEM((HEAD_ROWS, STATE_DEV), BF),
                pltpu.VMEM((CELL_NODES, NTYPE, CELL_NODES), BF),
                pltpu.SMEM(cell_type.shape, jnp.int32),
                pltpu.SMEM(atom_center.shape, jnp.int32),
                pltpu.VMEM(proj_values.shape, BF),
                pltpu.VMEM(coupling.shape, F32),
                pltpu.VMEM((1, STATE_DEV), F32),
                pltpu.VMEM((CELL_DEV, WIDE_ROWS, DEPTH), F32),
                pltpu.VMEM((CELL_DEV, ROWS, DEPTH), BF),
                pltpu.VMEM((CELL_DEV, COEFS, DEPTH), BF),
                pltpu.VMEM((CELL_DEV, 3 * COEFS + 2 * SIDE, DEPTH), BF),
                pltpu.VMEM((2, 2 * COEFS, DEPTH), BF),
                pltpu.VMEM((2, COEFS, DEPTH + 128), BF),
                pltpu.VMEM((2, COEFS, DEPTH + 128), BF),
                pltpu.VMEM((STRIDE + DEPTH + 2, 4 * COEFS), F32),
                pltpu.VMEM((BLOCK, 4 * COEFS), BF),
                pltpu.VMEM((2, 128, 2 * COEFS), F32),
                pltpu.VMEM((2, COEFS, 2 * COEFS), BF),
                pltpu.VMEM((STEPS, FIELD, STATE_DEV), F32),
                pltpu.VMEM((BLOCK, STATE_DEV), F32),
                pltpu.VMEM((STEPS, 2, NEAR_ROWS, STATE_DEV), F32),
                pltpu.VMEM((STEPS, 2, NEAR_ROWS, STATE_DEV), F32),
                pltpu.VMEM((STEPS - 1, 2, SIDE, STATE_DEV), F32),
                pltpu.VMEM((COEFS, STATE_DEV), BF),
                pltpu.VMEM((2, COEFS, STATE_DEV), BF),
                pltpu.VMEM((5, 128), F32),
                pltpu.VMEM((ns, 5, 128), F32),
                dma((7,)),
                dma((2, 2)),
                dma((2, 2)),
                dma((STEPS, 2, 2)),
                dma((2, 2)),
                dma((STEPS - 1, 2, 2)),
                dma((STEPS - 1, 2, 2)),
                dma((2, ns - 1)),
                pltpu.SemaphoreType.REGULAR((2,)),
            ],
            compiler_params=pltpu.CompilerParams(collective_id=0, has_side_effects=True),
        )(
            filter_input,
            jnp.swapaxes(cell_table, 0, 1),
            cell_type,
            atom_center,
            proj_values,
            coupling,
            occupation.reshape(1, STATE_DEV),
        )
        return pl.pallas_call(
            store,
            out_shape=(
                jax.ShapeDtypeStruct((NODE_DEV, STATE_DEV), F32),
                jax.ShapeDtypeStruct((NODE_DEV,), F32),
            ),
            in_specs=[any_space, any_space],
            out_specs=(any_space, any_space),
            scratch_shapes=[dma((2,))],
        )(*(pltpu.with_memory_space_constraint(v, pltpu.VMEM) for v in (filtered, density)))

    in_specs = (
        P("cells", "states"),
        P(),
        P("cells"),
        P("cells"),
        P("cells", None, None, None),
        P(),
        P("states"),
    )
    out_specs = (P("cells", "states"), P("cells"))
    return jax.shard_map(body, mesh=mesh, in_specs=in_specs, out_specs=out_specs, check_vma=False)
```
